512 devices in a mesh: ctx: 64 (over z_hi, x, y, core), pair: 8 (over z_lo).
Axes of the slice: x: 4, y: 4, z: 16 (z_hi: 2, z_lo: 8; z = z_hi * 8 + z_lo), core: 2. Of those that a mesh axis runs over, the one named last changes fastest.
Arguments:
- tokens: bfloat16 [8, 8192, 1536], P('pair', 'ctx'), may hold values from -24 to 24
- w_query: bfloat16 [1536, 512], P('pair'), may hold values from -0.15625 to 0.15625
- w_key: bfloat16 [1536, 128], P('pair'), may hold values from -0.15625 to 0.15625
- w_value: bfloat16 [1536, 192], P('pair'), may hold values from -0.15625 to 0.15625
- w_out: bfloat16 [768, 1536], P('pair'), may hold values from -0.21875 to 0.21875
- norm_gain: float32 [1536], replicated, may hold values from 0.5 to 1.5
- w_pair: bfloat16 [1536, 256], replicated, may hold values from -0.15625 to 0.15625
- conv_weight: bfloat16 [9, 128, 128], replicated, may hold values from -0.1875 to 0.1875
Outputs:
- seq_out: bfloat16 [8, 8192, 1536], P('pair', 'ctx')
- pair_out: bfloat16 [8, 512, 512, 128], P(None, 'ctx', 'pair')
The draws below stay inside these ranges and needn't reach their ends.
All inputs are finite; a program needn't handle non-finite values.
Results may differ from the reference program's by a relative error of at most 0.014.
The reference program's roundings to bfloat16 on the way count: a program that leaves them out, or rounds other values in their place, can miss the bound.
Values may be sent and summed in bfloat16 or wider, within the bound.
A program may use at most 128 MiB of HBM per device.

```python
import jax
import jax.numpy as jnp
from jax import lax

D = 1536
H = 4
KEY = 128
VAL = 192
PC = 128
POOL = 16
DILATION_STEP = 2
LEN = 8192
SEQS = 8
PAIR_LENGTH = 512


def draw_tokens(key, part):
    values = 2.5 * jax.random.normal(key, (SEQS, LEN, D), jnp.float32)
    return jnp.clip(values, -24.0, 24.0).astype(jnp.bfloat16)


def levels(key, shape, pieces, least, high):
    level = 1.0
    for dim, parts in pieces:
        steps = jax.random.uniform(jax.random.fold_in(jax.random.fold_in(key, 6), dim), (parts,), jnp.float32, least / len(pieces), high / len(pieces))
        level = level * jnp.repeat(jnp.exp(steps), shape[dim] // parts).reshape((-1,) + (1,) * (len(shape) - 1 - dim))
    return level


def scatter_about(own_key, dims, scale, limit, shards=(), dtype=jnp.bfloat16):
    loudness = levels(own_key, dims, shards, -0.22, 0.18) if shards else 1.0
    values = jax.random.normal(own_key, dims, jnp.float32) * scale * loudness
    return jnp.minimum(jnp.maximum(values, -limit), limit).astype(dtype)


def setup_inputs(seed: int = 0) -> dict:
    arg_keys = jax.random.split(jax.random.key(seed), 9)
    tokens = draw_tokens(jax.random.fold_in(arg_keys[8], 71), 0)
    w_query = scatter_about(arg_keys[1], (D, H * KEY), D ** -0.5, 0.15625, ((0, 8),))
    w_key = scatter_about(arg_keys[2], (D, KEY), D ** -0.5, 0.15625, ((0, 8),))
    w_value = scatter_about(arg_keys[3], (D, VAL), D ** -0.5, 0.15625, ((0, 8),))
    w_out = scatter_about(arg_keys[4], (H * VAL, D), (H * VAL) ** -0.5, 0.21875, ((0, 8),))
    norm_gain = jnp.clip(1.0 + 0.1 * jax.random.normal(arg_keys[5], (D,), jnp.float32), 0.5, 1.5)
    w_pair = scatter_about(arg_keys[6], (D, 2 * PC), D ** -0.5, 0.15625)
    conv_weight = scatter_about(arg_keys[7], (9, PC, PC), (9 * PC) ** -0.5, 0.1875)
    return dict(tokens=tokens, w_query=w_query, w_key=w_key, w_value=w_value, w_out=w_out, norm_gain=norm_gain, w_pair=w_pair, conv_weight=conv_weight)


def attend_block(query_block, keys_all, values_all):
    scores = jnp.einsum('qhk,nk->hqn', query_block.astype(jnp.float32), keys_all.astype(jnp.float32)) * KEY ** (-0.5)
    highest = lax.optimization_barrier(jnp.max(scores, axis=-1, keepdims=True))
    weights = jnp.exp(scores - highest)
    totals = lax.optimization_barrier(jnp.sum(weights, axis=-1))
    rounded = lax.optimization_barrier(weights.astype(jnp.bfloat16)).astype(jnp.float32)
    mixed = jnp.einsum('hqn,nv->hqv', rounded, values_all.astype(jnp.float32)) / totals[..., None]
    mixed = jnp.transpose(mixed, (1, 0, 2)).reshape(query_block.shape[0], H * VAL)
    return mixed.astype(jnp.bfloat16)

def attend_sequence(inputs):
    queries, keys_all, values_all = inputs
    block_rows = min(1024, LEN)
    blocks = queries.reshape(LEN // block_rows, block_rows, H, KEY)
    mixed = lax.map(lambda query_block: attend_block(query_block, keys_all, values_all), blocks)
    return mixed.reshape(LEN, H * VAL)

def reference(tokens, w_query, w_key, w_value, w_out, norm_gain, w_pair, conv_weight):
    flat = tokens.reshape(SEQS * LEN, D)
    queries = jnp.dot(flat, w_query, preferred_element_type=jnp.float32).astype(jnp.bfloat16).reshape(SEQS, LEN, H, KEY)
    keys = jnp.dot(flat, w_key, preferred_element_type=jnp.float32).astype(jnp.bfloat16).reshape(SEQS, LEN, KEY)
    values = jnp.dot(flat, w_value, preferred_element_type=jnp.float32).astype(jnp.bfloat16).reshape(SEQS, LEN, VAL)
    mixed = lax.map(attend_sequence, (queries, keys, values))
    projected = jnp.dot(mixed.reshape(SEQS * LEN, H * VAL), w_out, preferred_element_type=jnp.float32)
    summed = tokens.astype(jnp.float32) + projected.reshape(SEQS, LEN, D)
    seq_out = summed.astype(jnp.bfloat16)
    pooled = lax.optimization_barrier(jnp.mean(summed.reshape(SEQS, PAIR_LENGTH, POOL, D), axis=2))
    normed = pooled * lax.rsqrt(lax.optimization_barrier(jnp.mean(pooled * pooled, axis=-1, keepdims=True)) + 1e-06) * norm_gain
    normed = normed.astype(jnp.bfloat16)
    both = jnp.dot(normed.reshape(SEQS * PAIR_LENGTH, D), w_pair, preferred_element_type=jnp.float32).astype(jnp.bfloat16)
    both = both.reshape(SEQS, PAIR_LENGTH, 2 * PC)
    rowpart = both[:, :, :PC]
    colpart = both[:, :, PC:]

    def convolve(inputs):
        row_side, col_side = inputs
        pairwise_grid = (row_side.astype(jnp.float32)[:, None, :] * col_side.astype(jnp.float32)[None, :, :]).astype(jnp.bfloat16)
        padded_map = jnp.pad(pairwise_grid, ((DILATION_STEP, DILATION_STEP), (DILATION_STEP, DILATION_STEP), (0, 0)))
        total = jnp.zeros((PAIR_LENGTH * PAIR_LENGTH, PC), jnp.float32)
        for row_offset in range(3):
            for column_offset in range(3):
                kernel_window = padded_map[row_offset * DILATION_STEP:row_offset * DILATION_STEP + PAIR_LENGTH, column_offset * DILATION_STEP:column_offset * DILATION_STEP + PAIR_LENGTH, :]
                total = total + jnp.dot(kernel_window.reshape(PAIR_LENGTH * PAIR_LENGTH, PC), conv_weight[row_offset * 3 + column_offset], preferred_element_type=jnp.float32)
        result = pairwise_grid.astype(jnp.float32) + jax.nn.gelu(total.reshape(PAIR_LENGTH, PAIR_LENGTH, PC))
        return result.astype(jnp.bfloat16)
    pair_out = lax.map(convolve, (rowpart, colpart))
    return (seq_out, pair_out)
```

```python
import functools

import jax
import jax.numpy as jnp
from jax import lax
from jax.experimental import pallas as pl
from jax.experimental.pallas import tpu as pltpu
from jax.sharding import PartitionSpec as P

H = 4
KEY = 128
VAL = 192
PC = 128
POOL = 16
MESH = pl.DeviceIdType.MESH
BF = jnp.bfloat16
F32 = jnp.float32
BR = 384
HB = BR // 2
VMEM_LIMIT = 60 * 1024 * 1024


def coords():
    c = lax.axis_index("ctx")
    p = lax.axis_index("pair")
    return c, p, c // 32, (c // 8) % 4, (c // 2) % 4, c % 2


def ctx_of(zh, x, y, core):
    return ((zh * 4 + x) * 4 + y) * 2 + core


def at_z(c, zh, p, d):
    z = (zh * 8 + p + d + 16) % 16
    return ((z // 8) * 32 + c % 32, z % 8)


def rcopy(src, dst, ssem, rsem, dev):
    return pltpu.make_async_remote_copy(
        src_ref=src, dst_ref=dst, send_sem=ssem, recv_sem=rsem, device_id=dev, device_id_type=MESH
    )


def enter(devs):
    barrier = pltpu.get_barrier_semaphore()
    for dev in devs:
        pl.semaphore_signal(barrier, inc=1, device_id=dev, device_id_type=MESH)
    pl.semaphore_wait(barrier, len(devs))


def weights_kernel(wk, wv, wq, wo, WK, WV, WQ, WO, ss, rs, ps, pr, ls):
    c, p, zh, x, y, h = coords()
    partner = (c + 1 - 2 * h, p)
    dirs = (1, -1)
    nxt = [at_z(c, zh, p, d) for d in dirs]
    enter(nxt + [partner])
    arrs = ((wk, WK), (wv, WV), (wq, WQ), (wo, WO))
    locs = []
    for i, (src, out) in enumerate(arrs):
        r = src.shape[0]
        cp = pltpu.make_async_copy(src, out.at[pl.ds(pl.multiple_of(p * r, r), r), :], ls.at[i])
        cp.start()
        locs.append(cp)

    def part(i, shard, lanes=None):
        src, out = arrs[i]
        r = src.shape[0]
        hr = r // 2
        row = pl.ds(pl.multiple_of(shard * r + h * hr, hr), hr)
        return out.at[row, :] if lanes is None else out.at[row, lanes]

    def last(di):
        if di == 0:
            return ((0, None), (2, pl.ds(0, 256)), (3, pl.ds(0, 768)))
        return ((1, None), (2, pl.ds(256, 256)), (3, pl.ds(768, 768)))

    sent = []
    for group in ((0, 1, 2), (3,)):
        for di, d in enumerate(dirs):
            for i in group:
                src, _ = arrs[i]
                hr = src.shape[0] // 2
                cp = rcopy(
                    src.at[pl.ds(pl.multiple_of(h * hr, hr), hr), :],
                    part(i, p),
                    ss.at[di, 0, i],
                    rs.at[di, 0, i],
                    nxt[di],
                )
                cp.start()
                sent.append(cp)
        for t in (1, 2, 3):
            for di, d in enumerate(dirs):
                shard = (p - d * t + 8) % 8
                for i in group:
                    here = part(i, shard)
                    rcopy(here, here, ss.at[di, t - 1, i], rs.at[di, t - 1, i], nxt[di]).wait_recv()
                    if t < 3:
                        cp = rcopy(here, here, ss.at[di, t, i], rs.at[di, t, i], nxt[di])
                        cp.start()
                        sent.append(cp)
                    else:
                        for j, lanes in last(di):
                            if j == i:
                                ref = part(i, shard, lanes)
                                cp = rcopy(ref, ref, ss.at[di, 3, i], rs.at[di, 3, i], nxt[di])
                                cp.start()
                                sent.append(cp)
                    k = (t - 1) * 2 + di
                    cp = rcopy(here, here, ps.at[k, i], pr.at[k, i], partner)
                    cp.start()
                    sent.append(cp)
        shard = (p + 4) % 8
        for i in group:
            for di in range(2):
                for j, lanes in last(di):
                    if j == i:
                        ref = part(i, shard, lanes)
                        rcopy(ref, ref, ss.at[di, 3, i], rs.at[di, 3, i], nxt[di]).wait_recv()
            here = part(i, shard)
            cp = rcopy(here, here, ps.at[6, i], pr.at[6, i], partner)
            cp.start()
            sent.append(cp)
    g = 1 - h
    for i, (src, out) in enumerate(arrs):
        r = src.shape[0]
        hr = r // 2
        for k in range(7):
            if k < 6:
                shard = (p - dirs[k % 2] * (k // 2 + 1) + 8) % 8
            else:
                shard = (p + 4) % 8
            ref = out.at[pl.ds(pl.multiple_of(shard * r + g * hr, hr), hr), :]
            rcopy(ref, ref, ps.at[k, i], pr.at[k, i], partner).wait_recv()
    for cp in sent:
        cp.wait_send()
    for cp in locs:
        cp.wait()


def gather_weights(wk, wv, wq, wo):
    anyspec = pl.BlockSpec(memory_space=pltpu.VMEM)
    outs = tuple(jax.ShapeDtypeStruct((8 * w.shape[0], w.shape[1]), BF) for w in (wk, wv, wq, wo))
    dma = pltpu.SemaphoreType.DMA
    return pl.pallas_call(
        weights_kernel,
        out_shape=outs,
        in_specs=[anyspec] * 4,
        out_specs=(anyspec,) * 4,
        scratch_shapes=[dma((2, 4, 4)), dma((2, 4, 4)), dma((7, 4)), dma((7, 4)), dma((4,))],
        compiler_params=pltpu.CompilerParams(
            collective_id=0, has_side_effects=True, vmem_limit_bytes=VMEM_LIMIT
        ),
        name="weights",
    )(wk, wv, wq, wo)


def project_kernel(tok, WK, WV, WQ, kv, q):
    t = tok[...]
    kv[0:128, :] = jnp.dot(t, WK[...], preferred_element_type=F32).astype(BF)
    v = jnp.dot(t, WV[...], preferred_element_type=F32)
    kv[128:256, :] = v[:, :128].astype(BF)
    lane = lax.broadcasted_iota(jnp.int32, (128, 64), 1)
    ones = jnp.where(lane == 0, 1.0, 0.0).astype(F32)
    kv[256:384, :] = jnp.concatenate([v[:, 128:192], ones], axis=1).astype(BF)
    qq = jnp.dot(t, WQ[...], preferred_element_type=F32).astype(BF)
    for h in range(H):
        q[h * 128 : (h + 1) * 128, :] = qq[:, h * KEY : (h + 1) * KEY]


def project(tok, WK, WV, WQ):
    vm = pl.BlockSpec(memory_space=pltpu.VMEM)
    return pl.pallas_call(
        project_kernel,
        out_shape=(jax.ShapeDtypeStruct((BR, 128), BF), jax.ShapeDtypeStruct((512, 128), BF)),
        in_specs=[vm] * 4,
        out_specs=(vm, vm),
        compiler_params=pltpu.CompilerParams(vmem_limit_bytes=VMEM_LIMIT),
        name="project",
    )(tok, WK, WV, WQ)


def kv_kernel(blk, OUT, relay, ss, rs, ps, pr, zs, zr, ls):
    c, p, zh, x, y, h = coords()
    partner = (c + 1 - 2 * h, p)

    def slot(g, da, db, core=None):
        core = h if core is None else core
        z = zh if g == 0 else 1 - zh
        xx = (x + da * (1 - core) + db * core + 8) % 4
        yy = (y + da * core + db * (1 - core) + 8) % 4
        return ctx_of(z, xx, yy, core)

    ap, am = (slot(0, 1, 0), p), (slot(0, -1, 0), p)
    bp, bm = (slot(0, 0, 1), p), (slot(0, 0, -1), p)
    zp, zm = at_z(c, zh, p, 4), at_z(c, zh, p, -4)
    enter([ap, am, bp, bm, zp, zm, partner])
    sent = []

    def start(src, dst, s, r, dev):
        cp = rcopy(src, dst, s, r, dev)
        cp.start()
        sent.append(cp)

    loc = pltpu.make_async_copy(blk, OUT.at[c], ls.at[0])
    loc.start()
    top, bot = pl.ds(0, HB), pl.ds(HB, HB)
    halves = (top, bot)
    DA = (0, -1, 1, 2)

    def whole(g, s, own):
        return blk if own else OUT.at[s]

    def half(s, k):
        return OUT.at[s, halves[k], :]

    def to_a(g, own):
        s = slot(g, 0, 0)
        src = whole(g, s, own)
        start(src, OUT.at[s], ss.at[20 * g], rs.at[20 * g], ap)
        start(src, OUT.at[s], ss.at[20 * g + 1], rs.at[20 * g + 1], am)

    def to_b(g, j, own=False):
        s = slot(g, DA[j], 0)
        src = whole(g, s, own)
        k = 20 * g + 4 + 4 * j
        start(src, OUT.at[s], ss.at[k], rs.at[k], bp)
        start(src, OUT.at[s], ss.at[k + 1], rs.at[k + 1], bm)

    def to_partner(g, j, m, own=False):
        s = slot(g, DA[j], DA[m])
        k = 16 * g + 4 * j + m
        start(whole(g, s, own), OUT.at[s], ps.at[k], pr.at[k], partner)

    def got(ref, k):
        rcopy(ref, ref, ss.at[k], rs.at[k], partner).wait_recv()

    def a_near(g):
        for j, k, dev, hf in ((1, 0, ap, 0), (2, 1, am, 1)):
            s = slot(g, DA[j], 0)
            got(OUT.at[s], 20 * g + k)
            start(half(s, hf), half(s, hf), ss.at[20 * g + 2 + hf], rs.at[20 * g + 2 + hf], dev)
            to_b(g, j)
            to_partner(g, j, 0)

    def a_far(g):
        s = slot(g, 2, 0)
        got(half(s, 0), 20 * g + 2)
        got(half(s, 1), 20 * g + 3)
        to_b(g, 3)
        to_partner(g, 3, 0)

    def b_near(g, j):
        base = 20 * g + 4 + 4 * j
        for m, k, dev, hf in ((1, 0, bp, 0), (2, 1, bm, 1)):
            s = slot(g, DA[j], DA[m])
            got(OUT.at[s], base + k)
            start(half(s, hf), half(s, hf), ss.at[base + 2 + hf], rs.at[base + 2 + hf], dev)
            to_partner(g, j, m)

    def b_far(g, j):
        base = 20 * g + 4 + 4 * j
        s = slot(g, DA[j], 2)
        got(half(s, 0), base + 2)
        got(half(s, 1), base + 3)
        to_partner(g, j, 3)

    to_a(0, True)
    start(blk.at[top, :], relay.at[0], zs.at[0], zr.at[0], zp)
    start(blk.at[bot, :], relay.at[1], zs.at[1], zr.at[1], zm)
    to_b(0, 0, True)
    to_partner(0, 0, 0, True)
    a_near(0)
    b_near(0, 0)
    a_far(0)
    o1 = at_z(c, zh, p, -4)[0]
    o2 = at_z(c, zh, p, 4)[0]
    rcopy(relay.at[0], relay.at[0], zs.at[0], zr.at[0], zp).wait_recv()
    start(relay.at[0], OUT.at[o1, top, :], zs.at[2], zr.at[2], zp)
    rcopy(relay.at[1], relay.at[1], zs.at[1], zr.at[1], zm).wait_recv()
    start(relay.at[1], OUT.at[o2, bot, :], zs.at[3], zr.at[3], zm)
    b_far(0, 0)
    b_near(0, 1)
    b_near(0, 2)
    other = slot(1, 0, 0)
    r0, r1 = half(other, 0), half(other, 1)
    rcopy(r0, r0, zs.at[2], zr.at[2], zp).wait_recv()
    rcopy(r1, r1, zs.at[3], zr.at[3], zm).wait_recv()
    to_a(1, False)
    to_b(1, 0)
    to_partner(1, 0, 0)
    b_near(0, 3)
    b_far(0, 1)
    b_far(0, 2)
    b_far(0, 3)
    a_near(1)
    b_near(1, 0)
    a_far(1)
    b_far(1, 0)
    for j in (1, 2, 3):
        b_near(1, j)
    for j in (1, 2, 3):
        b_far(1, j)
    for g in range(2):
        for j in range(4):
            for m in range(4):
                s = slot(g, DA[j], DA[m], 1 - h)
                k = 16 * g + 4 * j + m
                rcopy(OUT.at[s], OUT.at[s], ps.at[k], pr.at[k], partner).wait_recv()
    for cp in sent:
        cp.wait_send()
    loc.wait()


def gather_kv(blk):
    vm = pl.BlockSpec(memory_space=pltpu.VMEM)
    dma = pltpu.SemaphoreType.DMA
    return pl.pallas_call(
        kv_kernel,
        out_shape=jax.ShapeDtypeStruct((64, BR, 128), BF),
        in_specs=[vm],
        out_specs=vm,
        scratch_shapes=[
            pltpu.VMEM((2, HB, 128), BF),
            dma((40,)),
            dma((40,)),
            dma((32,)),
            dma((32,)),
            dma((4,)),
            dma((4,)),
            dma((1,)),
        ],
        compiler_params=pltpu.CompilerParams(
            collective_id=1, has_side_effects=True, vmem_limit_bytes=VMEM_LIMIT
        ),
        name="gather_kv",
    )(blk)


CHUNK = 8


def attend_kernel(q_ref, kv_ref, tok, WO, gain, wpair, seq, rows, cols, acc, mixed):
    scale = KEY ** (-0.5) * 1.4426950408889634

    def step(i, m):
        blk = kv_ref[pl.ds(i * CHUNK, CHUNK)]
        n = CHUNK * 128
        k = blk[:, 0:128, :].reshape(n, 128)
        v1 = blk[:, 128:256, :].reshape(n, 128)
        v2 = blk[:, 256:384, :].reshape(n, 128)
        v = jnp.concatenate([v1, v2], axis=1)
        s = lax.dot_general(q_ref[...], k, (((1,), (1,)), ((), ())), preferred_element_type=F32)
        s = s * scale
        m2 = jnp.maximum(m, jnp.max(s, axis=1, keepdims=True))
        w = jnp.exp2(s - m2).astype(BF)
        o = jnp.dot(w, v, preferred_element_type=F32)
        acc[...] = acc[...] * jnp.exp2(m - m2) + o
        return m2

    acc[...] = jnp.zeros_like(acc)
    lax.fori_loop(0, 64 // CHUNK, step, jnp.full((512, 1), -1e30, F32))
    a = acc[...]
    mx = (a[:, 0:VAL] / a[:, VAL : VAL + 1]).astype(BF)
    for h in range(H):
        mixed[:, h * VAL : (h + 1) * VAL] = mx[h * 128 : (h + 1) * 128, :]
    summed = tok[...].astype(F32) + jnp.dot(mixed[...], WO[...], preferred_element_type=F32)
    seq[...] = summed.astype(BF)
    pooled = jnp.mean(summed.reshape(8, POOL, summed.shape[1]), axis=1)
    ms = jnp.mean(pooled * pooled, axis=-1, keepdims=True)
    normed = (pooled * lax.rsqrt(ms + 1e-06) * gain[...]).astype(BF)
    both = jnp.dot(normed, wpair[...], preferred_element_type=F32).astype(BF)
    rows[...] = both[:, :PC]
    cols[...] = both[:, PC:]


def attend(q, kv, tok, WO, gain, wpair):
    vm = pl.BlockSpec(memory_space=pltpu.VMEM)
    return pl.pallas_call(
        attend_kernel,
        out_shape=(
            jax.ShapeDtypeStruct(tok.shape, BF),
            jax.ShapeDtypeStruct((8, PC), BF),
            jax.ShapeDtypeStruct((8, PC), BF),
        ),
        in_specs=[vm] * 6,
        out_specs=(vm,) * 3,
        scratch_shapes=[pltpu.VMEM((512, 256), F32), pltpu.VMEM((128, H * VAL), BF)],
        compiler_params=pltpu.CompilerParams(vmem_limit_bytes=VMEM_LIMIT),
        name="attend",
    )(q, kv, tok, WO, gain, wpair)


def pair_kernel(rb, cb, RB, CB, HM, HL, HR, rs_s, rs_r, z_s, z_r, x_s, x_r, y_s, y_r, ls):
    c, p, zh, x, y, h = coords()
    flip = c + 32 - 64 * zh
    cn, cv = (c + 1) % 64, (c + 63) % 64
    pp = [(p + k) % 8 for k in range(8)]
    devs = [(c, pp[k]) for k in range(1, 8)] + [(flip, q) for q in range(8)]
    devs += [(cn, q) for q in range(8)] + [(cv, q) for q in range(8)]
    xs = [(ctx_of(zh, (x + k) % 4, y, h), p) for k in (1, 2, 3)]
    yc = []
    for k in range(4):
        for e in range(2):
            if k or e:
                yc.append((ctx_of(zh, x, (y + k) % 4, (h + e) % 2), p))
    enter(devs + xs + yc)

    def local(src, dst, k):
        cp = pltpu.make_async_copy(src, dst, ls.at[k])
        cp.start()
        cp.wait()

    tgt = c // 8
    jobs = [(tgt, HM, 0, None), (tgt + 1, HL, 1, (c % 8 == 7) & (tgt < 7)), (tgt - 1, HR, 2, (c % 8 == 0) & (tgt > 0))]

    def cond(pred, fn):
        if pred is None:
            fn()
        else:
            pl.when(pred)(fn)

    def col_sends(wait):
        for t, buf, b, pred in jobs:
            for f in range(2):
                dc = c if f == 0 else flip

                def go(t=t, buf=buf, b=b, f=f, dc=dc):
                    cp = rcopy(cb, buf.at[p], z_s.at[b, f], z_r.at[b, p], (dc, t))
                    cp.wait_send() if wait else cp.start()

                if f == 1:
                    cond(pred, go)
                else:
                    away = t != p
                    cond(away if pred is None else away & pred, go)

    col_sends(False)
    for t, buf, b, pred in jobs:
        mine = (t == p) if pred is None else (t == p) & pred
        pl.when(mine)(functools.partial(local, cb, buf.at[p], b))

    def row_sends(wait):
        for k in range(1, 8):
            cp = rcopy(rb, RB.at[1, p], rs_s.at[1, k], rs_r.at[1, p], (c, pp[k]))
            cp.wait_send() if wait else cp.start()
        for b, dc, pred in ((0, cn, c < 63), (2, cv, c > 0)):

            @pl.when(pred)
            def _():
                for k in range(8):
                    cp = rcopy(rb, RB.at[b, p], rs_s.at[b, k], rs_r.at[b, p], (dc, pp[k]))
                    cp.wait_send() if wait else cp.start()

    row_sends(False)
    local(rb, RB.at[1, p], 3)

    @pl.when(c == 0)
    def _():
        RB[0] = jnp.zeros((8, 8, PC), BF)

    @pl.when(c == 63)
    def _():
        RB[2] = jnp.zeros((8, 8, PC), BF)

    @pl.when(p == 0)
    def _():
        CB[0] = jnp.zeros((8, 8, PC), BF)

    @pl.when(p == 7)
    def _():
        CB[9] = jnp.zeros((8, 8, PC), BF)

    def spread(buf, b, owner, member, cslot):
        ox = owner % 4
        oz = owner // 4
        holder = member & (x == ox)

        @pl.when(holder)
        def _():
            for s in range(8):

                @pl.when((s != p) | (zh != oz))
                def _():
                    rcopy(buf.at[s], buf.at[s], z_s.at[b, 0], z_r.at[b, s], (c, p)).wait_recv()

            for k in range(3):
                rcopy(buf, buf, x_s.at[b, k], x_r.at[b], xs[k]).start()

        @pl.when(member & (x != ox))
        def _():
            rcopy(buf, buf, x_s.at[b, 0], x_r.at[b], (c, p)).wait_recv()

        @pl.when(member)
        def _():
            for k in range(7):
                rcopy(buf, CB.at[cslot], y_s.at[b, k], y_r.at[cslot], yc[k]).start()
            local(buf, CB.at[cslot], 4 + b)
            for k in range(7):
                rcopy(buf, CB.at[cslot], y_s.at[b, k], y_r.at[cslot], yc[k]).wait_send()

        @pl.when(holder)
        def _():
            for k in range(3):
                rcopy(buf, buf, x_s.at[b, k], x_r.at[b], xs[k]).wait_send()

    always = c >= 0
    mine = 1 + 2 * y + h
    lmem = (y == 3) & (h == 1) & (p > 0)
    rmem = (y == 0) & (h == 0) & (p < 7)
    spread(HM, 0, p, always, mine)
    spread(HL, 1, p - 1, lmem, 0)
    spread(HR, 2, p + 1, rmem, 9)

    for k in range(8):

        @pl.when(mine != k + 1)
        def _():
            rcopy(CB.at[k + 1], CB.at[k + 1], y_s.at[0, 0], y_r.at[k + 1], (c, p)).wait_recv()

    @pl.when((p > 0) & jnp.logical_not((y == 3) & (h == 1)))
    def _():
        rcopy(CB.at[0], CB.at[0], y_s.at[0, 0], y_r.at[0], (c, p)).wait_recv()

    @pl.when((p < 7) & jnp.logical_not((y == 0) & (h == 0)))
    def _():
        rcopy(CB.at[9], CB.at[9], y_s.at[0, 0], y_r.at[9], (c, p)).wait_recv()

    for k in range(1, 8):
        rcopy(RB.at[1, pp[k]], RB.at[1, pp[k]], rs_s.at[1, 1], rs_r.at[1, pp[k]], (c, p)).wait_recv()
    for b, pred in ((0, c > 0), (2, c < 63)):

        @pl.when(pred)
        def _():
            for k in range(8):
                rcopy(RB.at[b, k], RB.at[b, k], rs_s.at[b, 0], rs_r.at[b, k], (c, p)).wait_recv()

    row_sends(True)
    col_sends(True)


def exchange(rb, cb):
    vm = pl.BlockSpec(memory_space=pltpu.VMEM)
    dma = pltpu.SemaphoreType.DMA
    hold = pltpu.VMEM((8, 8, PC), BF)
    return pl.pallas_call(
        pair_kernel,
        out_shape=(jax.ShapeDtypeStruct((3, 8, 8, PC), BF), jax.ShapeDtypeStruct((10, 8, 8, PC), BF)),
        in_specs=[vm] * 2,
        out_specs=(vm,) * 2,
        scratch_shapes=[
            hold,
            hold,
            hold,
            dma((3, 8)),
            dma((3, 8)),
            dma((3, 2)),
            dma((3, 8)),
            dma((3, 3)),
            dma((3,)),
            dma((3, 7)),
            dma((10,)),
            dma((7,)),
        ],
        compiler_params=pltpu.CompilerParams(
            collective_id=2, has_side_effects=True, vmem_limit_bytes=VMEM_LIMIT
        ),
        name="exchange",
    )(rb, cb)


def conv_kernel(rb, cb, w, out):
    def seq(s, carry):
        prev = rb[0, pl.ds(s, 1)].reshape(8, PC).astype(F32)
        own = rb[1, pl.ds(s, 1)].reshape(8, PC).astype(F32)
        nxt = rb[2, pl.ds(s, 1)].reshape(8, PC).astype(F32)
        col = jnp.concatenate([cb[k, pl.ds(s, 1)].reshape(8, PC) for k in range(10)], axis=0).astype(F32)
        rows = [prev[6:7], prev[7:8]] + [own[k : k + 1] for k in range(8)] + [nxt[0:1], nxt[1:2]]
        shifted = [col[6 + 2 * b : 70 + 2 * b] for b in range(3)]
        maps = [[(r * cs).astype(BF) for r in rows] for cs in shifted]
        for i in range(8):
            lhs = jnp.concatenate(
                [maps[b][i + 2 * a] for a in range(3) for b in range(3)], axis=1
            )
            t = jnp.dot(lhs, w[...], preferred_element_type=F32)
            res = maps[1][i + 2].astype(F32) + jax.nn.gelu(t)
            out[pl.ds(s, 1), i] = res.astype(BF).reshape(1, 64, PC)
        return carry

    lax.fori_loop(0, 8, seq, 0)


def convolve(rb, cb, w):
    vm = pl.BlockSpec(memory_space=pltpu.VMEM)
    return pl.pallas_call(
        conv_kernel,
        out_shape=jax.ShapeDtypeStruct((8, 8, 64, PC), BF),
        in_specs=[vm] * 3,
        out_specs=vm,
        compiler_params=pltpu.CompilerParams(vmem_limit_bytes=VMEM_LIMIT),
        name="convolve",
    )(rb, cb, w)


def on_device(tokens, w_query, w_key, w_value, w_out, norm_gain, w_pair, conv_weight):
    tok = tokens.reshape(tokens.shape[1], tokens.shape[2])
    WK, WV, WQ, WO = gather_weights(w_key, w_value, w_query, w_out)
    blk, q = project(tok, WK, WV, WQ)
    kv = gather_kv(blk)
    seq, rows, cols = attend(q, kv, tok, WO, norm_gain.reshape(1, -1), w_pair)
    rb, cb = exchange(rows, cols)
    out = convolve(rb, cb, conv_weight.reshape(9 * PC, PC))
    return seq.reshape(tokens.shape), out


def solution(mesh):
    return jax.shard_map(
        on_device,
        mesh=mesh,
        in_specs=(
            P("pair", "ctx", None),
            P("pair", None),
            P("pair", None),
            P("pair", None),
            P("pair", None),
            P(),
            P(),
            P(),
        ),
        out_specs=(P("pair", "ctx", None), P(None, "ctx", "pair", None)),
        check_vma=False,
    )
```

```python
import functools

import jax
import jax.numpy as jnp
from jax import lax
from jax.experimental import pallas as pl
from jax.experimental.pallas import tpu as pltpu
from jax.sharding import PartitionSpec as P

H = 4
KEY = 128
VAL = 192
PC = 128
POOL = 16
MESH = pl.DeviceIdType.MESH
BF = jnp.bfloat16
F32 = jnp.float32
BR = 320
HB = BR // 2
VMEM_LIMIT = 60 * 1024 * 1024


def coords():
    c = lax.axis_index("ctx")
    p = lax.axis_index("pair")
    return c, p, c // 32, (c // 8) % 4, (c // 2) % 4, c % 2


def ctx_of(zh, x, y, core):
    return ((zh * 4 + x) * 4 + y) * 2 + core


def at_z(c, zh, p, d):
    z = (zh * 8 + p + d + 16) % 16
    return ((z // 8) * 32 + c % 32, z % 8)


def rcopy(src, dst, ssem, rsem, dev):
    return pltpu.make_async_remote_copy(
        src_ref=src, dst_ref=dst, send_sem=ssem, recv_sem=rsem, device_id=dev, device_id_type=MESH
    )


def enter(devs):
    barrier = pltpu.get_barrier_semaphore()
    for dev in devs:
        pl.semaphore_signal(barrier, inc=1, device_id=dev, device_id_type=MESH)
    pl.semaphore_wait(barrier, len(devs))


def exchange(rb, cb, RB, CB, HM, HL, HR, rs_s, rs_r, z_s, z_r, x_s, x_r, y_s, y_r, ls):
    c, p, zh, x, y, h = coords()
    flip = c + 32 - 64 * zh
    cn, cv = (c + 1) % 64, (c + 63) % 64
    pp = [(p + k) % 8 for k in range(8)]
    xs = [(ctx_of(zh, (x + k) % 4, y, h), p) for k in (1, 2, 3)]
    yc = []
    for k in range(4):
        for e in range(2):
            if k or e:
                yc.append((ctx_of(zh, x, (y + k) % 4, (h + e) % 2), p))

    def local(src, dst, k):
        cp = pltpu.make_async_copy(src, dst, ls.at[k])
        cp.start()
        cp.wait()

    tgt = c // 8
    jobs = [(tgt, HM, 0, None), (tgt + 1, HL, 1, (c % 8 == 7) & (tgt < 7)), (tgt - 1, HR, 2, (c % 8 == 0) & (tgt > 0))]

    def cond(pred, fn):
        if pred is None:
            fn()
        else:
            pl.when(pred)(fn)

    def col_sends(wait):
        for t, buf, b, pred in jobs:
            for f in range(2):
                dc = c if f == 0 else flip

                def go(t=t, buf=buf, b=b, f=f, dc=dc):
                    cp = rcopy(cb, buf.at[p], z_s.at[b, f], z_r.at[b, p], (dc, t))
                    cp.wait_send() if wait else cp.start()

                if f == 1:
                    cond(pred, go)
                else:
                    away = t != p
                    cond(away if pred is None else away & pred, go)

    col_sends(False)
    for t, buf, b, pred in jobs:
        mine = (t == p) if pred is None else (t == p) & pred
        pl.when(mine)(functools.partial(local, cb, buf.at[p], b))

    def row_sends(wait):
        for k in range(1, 8):
            cp = rcopy(rb, RB.at[1, p], rs_s.at[1, k], rs_r.at[1, p], (c, pp[k]))
            cp.wait_send() if wait else cp.start()
        for b, dc, pred in ((0, cn, c < 63), (2, cv, c > 0)):

            @pl.when(pred)
            def _():
                for k in range(8):
                    cp = rcopy(rb, RB.at[b, p], rs_s.at[b, k], rs_r.at[b, p], (dc, pp[k]))
                    cp.wait_send() if wait else cp.start()

    row_sends(False)
    local(rb, RB.at[1, p], 3)

    @pl.when(c == 0)
    def _():
        RB[0] = jnp.zeros((8, 8, PC), BF)

    @pl.when(c == 63)
    def _():
        RB[2] = jnp.zeros((8, 8, PC), BF)

    @pl.when(p == 0)
    def _():
        CB[0] = jnp.zeros((8, 8, PC), BF)

    @pl.when(p == 7)
    def _():
        CB[9] = jnp.zeros((8, 8, PC), BF)

    def spread(buf, b, owner, member, cslot):
        ox = owner % 4
        oz = owner // 4
        holder = member & (x == ox)

        @pl.when(holder)
        def _():
            for s in range(8):

                @pl.when((s != p) | (zh != oz))
                def _():
                    rcopy(buf.at[s], buf.at[s], z_s.at[b, 0], z_r.at[b, s], (c, p)).wait_recv()

            for k in range(3):
                rcopy(buf, buf, x_s.at[b, k], x_r.at[b], xs[k]).start()

        @pl.when(member & (x != ox))
        def _():
            rcopy(buf, buf, x_s.at[b, 0], x_r.at[b], (c, p)).wait_recv()

        @pl.when(member)
        def _():
            for k in range(7):
                rcopy(buf, CB.at[cslot], y_s.at[b, k], y_r.at[cslot], yc[k]).start()
            local(buf, CB.at[cslot], 4 + b)
            for k in range(7):
                rcopy(buf, CB.at[cslot], y_s.at[b, k], y_r.at[cslot], yc[k]).wait_send()

        @pl.when(holder)
        def _():
            for k in range(3):
                rcopy(buf, buf, x_s.at[b, k], x_r.at[b], xs[k]).wait_send()

    always = c >= 0
    mine = 1 + 2 * y + h
    lmem = (y == 3) & (h == 1) & (p > 0)
    rmem = (y == 0) & (h == 0) & (p < 7)
    spread(HM, 0, p, always, mine)
    spread(HL, 1, p - 1, lmem, 0)
    spread(HR, 2, p + 1, rmem, 9)

    for k in range(8):

        @pl.when(mine != k + 1)
        def _():
            rcopy(CB.at[k + 1], CB.at[k + 1], y_s.at[0, 0], y_r.at[k + 1], (c, p)).wait_recv()

    @pl.when((p > 0) & jnp.logical_not((y == 3) & (h == 1)))
    def _():
        rcopy(CB.at[0], CB.at[0], y_s.at[0, 0], y_r.at[0], (c, p)).wait_recv()

    @pl.when((p < 7) & jnp.logical_not((y == 0) & (h == 0)))
    def _():
        rcopy(CB.at[9], CB.at[9], y_s.at[0, 0], y_r.at[9], (c, p)).wait_recv()

    for k in range(1, 8):
        rcopy(RB.at[1, pp[k]], RB.at[1, pp[k]], rs_s.at[1, 1], rs_r.at[1, pp[k]], (c, p)).wait_recv()
    for b, pred in ((0, c > 0), (2, c < 63)):

        @pl.when(pred)
        def _():
            for k in range(8):
                rcopy(RB.at[b, k], RB.at[b, k], rs_s.at[b, 0], rs_r.at[b, k], (c, p)).wait_recv()

    row_sends(True)
    col_sends(True)


class Net:
    def __init__(self):
        self.sent = []

    def start(self, src, dst, s, r, dev):
        cp = rcopy(src, dst, s, r, dev)
        cp.start()
        self.sent.append(cp)

    def finish(self):
        for cp in self.sent:
            cp.wait_send()


class Ring:
    def __init__(self, net, arrs, place, ss, rs, ps, pr):
        self.net, self.arrs = net, arrs
        self.c, self.p, zh, _, _, self.h = place
        self.partner = (self.c + 1 - 2 * self.h, self.p)
        self.nxt = [at_z(self.c, zh, self.p, d) for d in (1, -1)]
        self.ss, self.rs, self.ps, self.pr = ss, rs, ps, pr

    def part(self, i, shard, lanes=None, h=None):
        src, out = self.arrs[i]
        h = self.h if h is None else h
        r = src.shape[0]
        hr = r // 2
        row = pl.ds(pl.multiple_of(shard * r + h * hr, hr), hr)
        return out.at[row, :] if lanes is None else out.at[row, lanes]

    def shard(self, t, di):
        return (self.p - t * (1, -1)[di] + 8) % 8

    def last(self, i, di):
        if i == di:
            return pl.ds(0, self.arrs[i][0].shape[1])
        if i < 2:
            return None
        w = self.arrs[i][0].shape[1] // 2
        return pl.ds(di * w, w)

    def first(self, i):
        src, _ = self.arrs[i]
        hr = src.shape[0] // 2
        for di in range(2):
            self.net.start(
                src.at[pl.ds(pl.multiple_of(self.h * hr, hr), hr), :],
                self.part(i, self.p),
                self.ss.at[di, 0, i],
                self.rs.at[di, 0, i],
                self.nxt[di],
            )

    def got(self, ref, s, r):
        rcopy(ref, ref, s, r, self.partner).wait_recv()

    def hop(self, i, t):
        for di in range(2):
            here = self.part(i, self.shard(t, di))
            self.got(here, self.ss.at[di, t - 1, i], self.rs.at[di, t - 1, i])
            ref = here
            if t == 3:
                lanes = self.last(i, di)
                ref = None if lanes is None else self.part(i, self.shard(t, di), lanes)
            if ref is not None:
                self.net.start(ref, ref, self.ss.at[di, t, i], self.rs.at[di, t, i], self.nxt[di])
            k = (t - 1) * 2 + di
            self.net.start(here, here, self.ps.at[k, i], self.pr.at[k, i], self.partner)

    def far(self, i):
        for di in range(2):
            lanes = self.last(i, di)
            if lanes is not None:
                ref = self.part(i, self.shard(4, 0), lanes)
                self.got(ref, self.ss.at[di, 3, i], self.rs.at[di, 3, i])
        here = self.part(i, self.shard(4, 0))
        self.net.start(here, here, self.ps.at[6, i], self.pr.at[6, i], self.partner)

    def done(self, i):
        for k in range(7):
            shard = self.shard(k // 2 + 1, k % 2) if k < 6 else self.shard(4, 0)
            ref = self.part(i, shard, h=1 - self.h)
            self.got(ref, self.ps.at[k, i], self.pr.at[k, i])


class Gather:
    def __init__(self, net, kv, place, ss, rs, ps, pr):
        self.net, self.kv = net, kv
        c, p, zh, x, y, h = place
        self.ss, self.rs, self.ps, self.pr = ss, rs, ps, pr
        self.partner = (c + 1 - 2 * h, p)
        self.ap = (ctx_of(zh, (x + 1 - h) % 4, (y + h) % 4, h), p)
        self.am = (ctx_of(zh, (x + 3 + h) % 4, (y + 4 - h) % 4, h), p)
        self.bp = (ctx_of(zh, (x + h) % 4, (y + 1 - h) % 4, h), p)
        self.bm = (ctx_of(zh, (x + 4 - h) % 4, (y + 3 + h) % 4, h), p)

    def slot(self, g, j, m, r=0):
        return self.kv.at[((g * 4 + j) * 2 + r) * 4 + m]

    def half(self, g, j, m, k):
        return self.kv.at[((g * 4 + j) * 2) * 4 + m, pl.ds(k * HB, HB), :]

    def got(self, ref, k):
        rcopy(ref, ref, self.ss.at[k], self.rs.at[k], self.partner).wait_recv()

    def send(self, src, dst, k, dev):
        self.net.start(src, dst, self.ss.at[k], self.rs.at[k], dev)

    def to_b(self, g, j, src=None):
        src = self.slot(g, j, 0) if src is None else src
        k = 20 * g + 4 + 4 * j
        self.send(src, self.slot(g, j, 1), k, self.bp)
        self.send(src, self.slot(g, j, 2), k + 1, self.bm)

    def to_partner(self, g, j, m, src=None):
        src = self.slot(g, j, m) if src is None else src
        k = 16 * g + 4 * j + m
        self.net.start(src, self.slot(g, j, m, 1), self.ps.at[k], self.pr.at[k], self.partner)

    def own(self, g, src=None):
        a = self.slot(g, 0, 0) if src is None else src
        self.send(a, self.slot(g, 1, 0), 20 * g, self.ap)
        self.send(a, self.slot(g, 2, 0), 20 * g + 1, self.am)
        self.to_b(g, 0, src)
        self.to_partner(g, 0, 0, src)

    def a_near(self, g):
        for j, k, dev in ((1, 0, self.ap), (2, 1, self.am)):
            self.got(self.slot(g, j, 0), 20 * g + k)
            self.send(self.half(g, j, 0, k), self.half(g, 3, 0, k), 20 * g + 2 + k, dev)
            self.to_b(g, j)
            self.to_partner(g, j, 0)

    def a_far(self, g):
        for k in range(2):
            self.got(self.half(g, 3, 0, k), 20 * g + 2 + k)
        self.to_b(g, 3)
        self.to_partner(g, 3, 0)

    def b_near(self, g, j):
        base = 20 * g + 4 + 4 * j
        for m, k, dev in ((1, 0, self.bp), (2, 1, self.bm)):
            self.got(self.slot(g, j, m), base + k)
            self.send(self.half(g, j, m, k), self.half(g, j, 3, k), base + 2 + k, dev)
            self.to_partner(g, j, m)

    def b_far(self, g, j):
        base = 20 * g + 4 + 4 * j
        for k in range(2):
            self.got(self.half(g, j, 3, k), base + 2 + k)
        self.to_partner(g, j, 3)

    def from_partner(self, g, j):
        for m in range(4):
            k = 16 * g + 4 * j + m
            ref = self.slot(g, j, m, 1)
            rcopy(ref, ref, self.ps.at[k], self.pr.at[k], self.partner).wait_recv()


def front_kernel(
    tok, wk, wv, wq, wo, gain, wpair,
    seq, RB, CB,
    WK, WV, WQ, WO, kv, blk, q, acc, high, mixed, rb, cb, HM, HL, HR,
    wss, wrs, wps, wpr, kss, krs, kps, kpr, zs, zr, ls, hello,
    rs_s, rs_r, z_s, z_r, x_s, x_r, y_s, y_r, els,
):
    place = coords()
    c, p, zh, x, y, h = place
    net = Net()
    arrs = ((wk, WK), (wv, WV), (wq, WQ), (wo, WO))
    ring = Ring(net, arrs, place, wss, wrs, wps, wpr)
    kvs = Gather(net, kv, place, kss, krs, kps, kpr)
    enter(ring.nxt + [ring.partner, kvs.ap, kvs.am, kvs.bp, kvs.bm])
    for i in range(3):
        ring.first(i)
    locs = []
    for i, (src, out) in enumerate(arrs):
        r = src.shape[0]
        cp = pltpu.make_async_copy(src, out.at[pl.ds(pl.multiple_of(p * r, r), r), :], ls.at[i])
        cp.start()
        locs.append(cp)

    for t in (1, 2, 3):
        ring.hop(0, t)
        ring.hop(1, t)
    ring.far(0)
    ring.far(1)
    pl.semaphore_signal(hello, inc=1, device_id=at_z(c, zh, p, -4), device_id_type=MESH)
    ring.hop(2, 1)
    locs[0].wait()
    locs[1].wait()
    ring.done(0)
    ring.done(1)
    t = tok[...]
    blk[0:128, :] = jnp.dot(t, WK[...], preferred_element_type=F32).astype(BF)
    v = jnp.dot(t, WV[...], preferred_element_type=F32)
    blk[128:256, :] = v[:, :128].astype(BF)
    blk[256:320, :] = jnp.concatenate([v[0:64, 128:192], v[64:128, 128:192]], axis=1).astype(BF)

    kvs.own(0, blk)
    loc = pltpu.make_async_copy(blk, kvs.slot(0, 0, 0), ls.at[4])
    loc.start()
    pl.semaphore_wait(hello, 1)
    flip = (c + 32 - 64 * zh, p)
    net.start(blk, kvs.slot(1, 0, 0), zs, zr, flip)
    ring.first(3)
    ring.hop(2, 2)
    kvs.a_near(0)
    kvs.b_near(0, 0)
    ring.hop(2, 3)
    kvs.a_far(0)
    kvs.b_far(0, 0)
    kvs.b_near(0, 1)
    kvs.b_near(0, 2)
    ring.far(2)
    ring.hop(3, 1)
    kvs.b_near(0, 3)
    for j in (1, 2, 3):
        kvs.b_far(0, j)
    locs[2].wait()
    ring.done(2)
    qq = jnp.dot(tok[...], WQ[...], preferred_element_type=F32).astype(BF)
    for n in range(H):
        q[n * 128 : (n + 1) * 128, :] = qq[:, n * KEY : (n + 1) * KEY]
    acc[...] = jnp.zeros_like(acc)
    high[...] = jnp.full_like(high, -1e30)
    loc.wait()

    scale = KEY ** (-0.5) * 1.4426950408889634

    def attend(g, j):
        kvs.from_partner(g, j)
        part = kv[pl.ds((g * 4 + j) * 8, 8)]
        k = part[:, 0:128, :].reshape(1024, 128)
        v1 = part[:, 128:256, :].reshape(1024, 128)
        lo = part[:, 256:320, :].astype(F32)
        hi = pltpu.roll(lo.reshape(512, 128), 64, 1).reshape(8, 64, 128)
        v2 = jnp.concatenate([lo, hi], axis=1).reshape(1024, 128)
        lane = lax.broadcasted_iota(jnp.int32, (1024, 128), 1)
        v2 = jnp.where(lane == 64, 1.0, v2).astype(BF)
        m = high[:, 0:1]
        s = lax.dot_general(q[...], k, (((1,), (1,)), ((), ())), preferred_element_type=F32)
        m2 = jnp.maximum(m, jnp.max(s, axis=1, keepdims=True))
        w = jnp.exp2((s - m2) * scale).astype(BF)
        o = jnp.dot(w, jnp.concatenate([v1, v2], axis=1), preferred_element_type=F32)
        acc[...] = acc[...] * jnp.exp2((m - m2) * scale) + o
        high[...] = jnp.broadcast_to(m2, high.shape)

    attend(0, 0)
    ring.hop(3, 2)
    other = kvs.slot(1, 0, 0)
    rcopy(other, other, zs, zr, flip).wait_recv()
    kvs.own(1)
    attend(0, 1)
    kvs.a_near(1)
    kvs.b_near(1, 0)
    ring.hop(3, 3)
    kvs.a_far(1)
    attend(0, 2)
    kvs.b_far(1, 0)
    kvs.b_near(1, 1)
    kvs.b_near(1, 2)
    kvs.b_near(1, 3)
    ring.far(3)
    attend(0, 3)
    for j in (1, 2, 3):
        kvs.b_far(1, j)
    for j in range(4):
        attend(1, j)
    locs[3].wait()
    ring.done(3)

    a = acc[...]
    mx = (a[:, 0:VAL] / a[:, VAL : VAL + 1]).astype(BF)
    for n in range(H):
        mixed[:, n * VAL : (n + 1) * VAL] = mx[n * 128 : (n + 1) * 128, :]
    summed = tok[...].astype(F32) + jnp.dot(mixed[...], WO[...], preferred_element_type=F32)
    seq[...] = summed.astype(BF)
    pooled = jnp.mean(summed.reshape(8, POOL, summed.shape[1]), axis=1)
    ms = jnp.mean(pooled * pooled, axis=-1, keepdims=True)
    normed = (pooled * lax.rsqrt(ms + 1e-06) * gain[...]).astype(BF)
    both = jnp.dot(normed, wpair[...], preferred_element_type=F32).astype(BF)
    rb[...] = both[:, :PC]
    cb[...] = both[:, PC:]
    exchange(rb, cb, RB, CB, HM, HL, HR, rs_s, rs_r, z_s, z_r, x_s, x_r, y_s, y_r, els)
    net.finish()


def front(tok, wk, wv, wq, wo, gain, wpair):
    vm = pl.BlockSpec(memory_space=pltpu.VMEM)
    dma = pltpu.SemaphoreType.DMA
    hold = pltpu.VMEM((8, 8, PC), BF)
    return pl.pallas_call(
        front_kernel,
        out_shape=(
            jax.ShapeDtypeStruct(tok.shape, BF),
            jax.ShapeDtypeStruct((3, 8, 8, PC), BF),
            jax.ShapeDtypeStruct((10, 8, 8, PC), BF),
        ),
        in_specs=[vm] * 7,
        out_specs=(vm,) * 3,
        scratch_shapes=[pltpu.VMEM((8 * w.shape[0], w.shape[1]), BF) for w in (wk, wv, wq, wo)]
        + [
            pltpu.VMEM((64, BR, 128), BF),
            pltpu.VMEM((BR, 128), BF),
            pltpu.VMEM((512, 128), BF),
            pltpu.VMEM((512, 256), F32),
            pltpu.VMEM((512, 128), F32),
            pltpu.VMEM((128, H * VAL), BF),
            pltpu.VMEM((8, PC), BF),
            pltpu.VMEM((8, PC), BF),
            hold,
            hold,
            hold,
        ]
        + [dma((2, 4, 4)), dma((2, 4, 4)), dma((7, 4)), dma((7, 4))]
        + [dma((40,)), dma((40,)), dma((32,)), dma((32,)), dma, dma, dma((5,))]
        + [pltpu.SemaphoreType.REGULAR]
        + [dma((3, 8)), dma((3, 8)), dma((3, 2)), dma((3, 8)), dma((3, 3)), dma((3,)), dma((3, 7)), dma((10,)), dma((7,))],
        compiler_params=pltpu.CompilerParams(
            collective_id=0, has_side_effects=True, vmem_limit_bytes=VMEM_LIMIT
        ),
        name="front",
    )(tok, wk, wv, wq, wo, gain, wpair)


def conv_kernel(rb, cb, w, seq_in, out, seq_out):
    seq_out[...] = seq_in[...]

    def seq(s, carry):
        prev = rb[0, pl.ds(s, 1)].reshape(8, PC).astype(F32)
        own = rb[1, pl.ds(s, 1)].reshape(8, PC).astype(F32)
        nxt = rb[2, pl.ds(s, 1)].reshape(8, PC).astype(F32)
        col = jnp.concatenate([cb[k, pl.ds(s, 1)].reshape(8, PC) for k in range(10)], axis=0).astype(F32)
        rows = [prev[6:7], prev[7:8]] + [own[k : k + 1] for k in range(8)] + [nxt[0:1], nxt[1:2]]
        shifted = [col[6 + 2 * b : 70 + 2 * b] for b in range(3)]
        maps = [[(r * cs).astype(BF) for r in rows] for cs in shifted]
        for i in range(8):
            lhs = jnp.concatenate(
                [maps[b][i + 2 * a] for a in range(3) for b in range(3)], axis=1
            )
            t = jnp.dot(lhs, w[...], preferred_element_type=F32)
            res = maps[1][i + 2].astype(F32) + jax.nn.gelu(t)
            out[pl.ds(s, 1), i] = res.astype(BF).reshape(1, 64, PC)
        return carry

    lax.fori_loop(0, 8, seq, 0)


def convolve(rb, cb, w, seq):
    vm = pl.BlockSpec(memory_space=pltpu.VMEM)
    return pl.pallas_call(
        conv_kernel,
        out_shape=(jax.ShapeDtypeStruct((8, 8, 64, PC), BF), jax.ShapeDtypeStruct(seq.shape, BF)),
        in_specs=[vm] * 4,
        out_specs=(vm, vm),
        compiler_params=pltpu.CompilerParams(vmem_limit_bytes=VMEM_LIMIT),
        name="convolve",
    )(rb, cb, w, seq)


def on_device(tokens, w_query, w_key, w_value, w_out, norm_gain, w_pair, conv_weight):
    tok = tokens.reshape(tokens.shape[1], tokens.shape[2])
    seq, rb, cb = front(tok, w_key, w_value, w_query, w_out, norm_gain.reshape(1, -1), w_pair)
    out, seq = convolve(rb, cb, conv_weight.reshape(9 * PC, PC), seq)
    return seq.reshape(tokens.shape), out


def solution(mesh):
    return jax.shard_map(
        on_device,
        mesh=mesh,
        in_specs=(
            P("pair", "ctx", None),
            P("pair", None),
            P("pair", None),
            P("pair", None),
            P("pair", None),
            P(),
            P(),
            P(),
        ),
        out_specs=(P("pair", "ctx", None), P(None, "ctx", "pair", None)),
        check_vma=False,
    )
```

```python
import functools

import jax
import jax.numpy as jnp
from jax import lax
from jax.experimental import pallas as pl
from jax.experimental.pallas import tpu as pltpu
from jax.sharding import PartitionSpec as P

H = 4
KEY = 128
VAL = 192
PC = 128
POOL = 16
MESH = pl.DeviceIdType.MESH
BF = jnp.bfloat16
F32 = jnp.float32
BR = 320
HB = BR // 2
VMEM_LIMIT = 60 * 1024 * 1024


def coords():
    c = lax.axis_index("ctx")
    p = lax.axis_index("pair")
    return c, p, c // 32, (c // 8) % 4, (c // 2) % 4, c % 2


def ctx_of(zh, x, y, core):
    return ((zh * 4 + x) * 4 + y) * 2 + core


def at_z(c, zh, p, d):
    z = (zh * 8 + p + d + 16) % 16
    return ((z // 8) * 32 + c % 32, z % 8)


def rcopy(src, dst, ssem, rsem, dev):
    return pltpu.make_async_remote_copy(
        src_ref=src, dst_ref=dst, send_sem=ssem, recv_sem=rsem, device_id=dev, device_id_type=MESH
    )


def enter(devs):
    barrier = pltpu.get_barrier_semaphore()
    for dev in devs:
        pl.semaphore_signal(barrier, inc=1, device_id=dev, device_id_type=MESH)
    pl.semaphore_wait(barrier, len(devs))


def exchange(rb, cb, RB, CB, HM, HL, HR, rs_s, rs_r, z_s, z_r, y_s, y_r, ls):
    c, p, zh, x, y, h = coords()
    cn, cv = (c + 1) % 64, (c + 63) % 64
    pp = [(p + k) % 8 for k in range(8)]
    yc = []
    for k in range(4):
        for e in range(2):
            if k or e:
                yc.append((ctx_of(zh, x, (y + k) % 4, (h + e) % 2), p))

    def local(src, dst, k):
        cp = pltpu.make_async_copy(src, dst, ls.at[k])
        cp.start()
        cp.wait()

    def cond(pred, fn):
        if pred is None:
            fn()
        else:
            pl.when(pred)(fn)

    tgt = c // 8
    jobs = [
        (tgt, HM, 0, None),
        (tgt + 1, HL, 1, (c % 8 == 7) & (tgt < 7)),
        (tgt - 1, HR, 2, (c % 8 == 0) & (tgt > 0)),
    ]

    def col_sends(wait):
        for t, buf, b, pred in jobs:
            for f in (1, 0):
                for k in (2, 1, 3, 0):
                    dc = ctx_of(zh if f == 0 else 1 - zh, (x + k) % 4, y, h)

                    def go(t=t, buf=buf, b=b, n=4 * f + k, dc=dc):
                        cp = rcopy(cb, buf.at[p], z_s.at[b, n], z_r.at[b, p], (dc, t))
                        cp.wait_send() if wait else cp.start()

                    if f or k:
                        cond(pred, go)
                    else:
                        away = t != p
                        cond(away if pred is None else away & pred, go)

    col_sends(False)
    for t, buf, b, pred in jobs:
        mine = (t == p) if pred is None else (t == p) & pred
        pl.when(mine)(functools.partial(local, cb, buf.at[p], b))

    def row_sends(wait):
        for k in range(1, 8):
            cp = rcopy(rb, RB.at[1, p], rs_s.at[1, k], rs_r.at[1, p], (c, pp[k]))
            cp.wait_send() if wait else cp.start()
        for b, dc, pred in ((0, cn, c < 63), (2, cv, c > 0)):

            @pl.when(pred)
            def _():
                for k in range(8):
                    cp = rcopy(rb, RB.at[b, p], rs_s.at[b, k], rs_r.at[b, p], (dc, pp[k]))
                    cp.wait_send() if wait else cp.start()

    row_sends(False)
    local(rb, RB.at[1, p], 3)

    @pl.when(c == 0)
    def _():
        RB[0] = jnp.zeros((8, 8, PC), BF)

    @pl.when(c == 63)
    def _():
        RB[2] = jnp.zeros((8, 8, PC), BF)

    @pl.when(p == 0)
    def _():
        CB[0] = jnp.zeros((8, 8, PC), BF)

    @pl.when(p == 7)
    def _():
        CB[9] = jnp.zeros((8, 8, PC), BF)

    mine = 1 + 2 * y + h
    spreads = (
        (HM, 0, p, None, mine),
        (HL, 1, p - 1, (y == 3) & (h == 1) & (p > 0), 0),
        (HR, 2, p + 1, (y == 0) & (h == 0) & (p < 7), 9),
    )
    for buf, b, owner, member, cslot in spreads:

        def take(buf=buf, b=b, owner=owner, cslot=cslot):
            for n in range(8):

                @pl.when((p != n) | (zh != owner // 4) | (x != owner % 4))
                def _():
                    rcopy(buf.at[n], buf.at[n], z_s.at[b, 0], z_r.at[b, n], (c, p)).wait_recv()

            for k in range(7):
                rcopy(buf, CB.at[cslot], y_s.at[b, k], y_r.at[cslot], yc[k]).start()
            local(buf, CB.at[cslot], 4 + b)

        cond(member, take)

    for k in range(8):

        @pl.when(mine != k + 1)
        def _():
            rcopy(CB.at[k + 1], CB.at[k + 1], y_s.at[0, 0], y_r.at[k + 1], (c, p)).wait_recv()

    @pl.when((p > 0) & jnp.logical_not((y == 3) & (h == 1)))
    def _():
        rcopy(CB.at[0], CB.at[0], y_s.at[0, 0], y_r.at[0], (c, p)).wait_recv()

    @pl.when((p < 7) & jnp.logical_not((y == 0) & (h == 0)))
    def _():
        rcopy(CB.at[9], CB.at[9], y_s.at[0, 0], y_r.at[9], (c, p)).wait_recv()

    for k in range(1, 8):
        rcopy(RB.at[1, pp[k]], RB.at[1, pp[k]], rs_s.at[1, 1], rs_r.at[1, pp[k]], (c, p)).wait_recv()
    for b, pred in ((0, c > 0), (2, c < 63)):

        @pl.when(pred)
        def _():
            for k in range(8):
                rcopy(RB.at[b, k], RB.at[b, k], rs_s.at[b, 0], rs_r.at[b, k], (c, p)).wait_recv()

    row_sends(True)
    col_sends(True)
    for buf, b, owner, member, cslot in spreads:

        def sent(buf=buf, b=b, cslot=cslot):
            for k in range(7):
                rcopy(buf, CB.at[cslot], y_s.at[b, k], y_r.at[cslot], yc[k]).wait_send()

        cond(member, sent)


class Net:
    def __init__(self):
        self.sent = []

    def start(self, src, dst, s, r, dev):
        cp = rcopy(src, dst, s, r, dev)
        cp.start()
        self.sent.append(cp)

    def finish(self):
        for cp in self.sent:
            cp.wait_send()


DIST = (1, -1, 2, -2, 3, -3, 4)


class Weights:
    def __init__(self, net, arrs, place, zs, zr, ns, nr, ps, pr):
        self.net, self.arrs = net, arrs
        self.c, self.p, self.zh, x, y, self.h = place
        self.color = (x + y) % 2
        self.partner = (self.c + 1 - 2 * self.h, self.p)
        self.plane = [
            (ctx_of(self.zh, (x + dx) % 4, (y + dy) % 4, self.h), self.p)
            for dx, dy in ((1, 0), (3, 0), (0, 1), (0, 3))
        ]
        self.zs, self.zr, self.ns, self.nr, self.ps, self.pr = zs, zr, ns, nr, ps, pr

    def at(self, d):
        return at_z(self.c, self.zh, self.p, d)

    def quarter(self, i, base, h, color, side=None):
        src, _ = self.arrs[i]
        r, w = src.shape
        if i < 3:
            n = r // 4
            row, lane, wide = base + h * 2 * n + color * n, 0, w
        else:
            n = r // 2
            row, lane, wide = base + h * n, pl.multiple_of(color * (w // 2), w // 2), w // 2
        if side is not None:
            wide = wide // 2
            lane = lane + side * wide
            if i == 3:
                lane = pl.multiple_of(lane, wide)
        return pl.ds(pl.multiple_of(row, n), n), pl.ds(lane, wide)

    def own(self, i, side=None):
        rows, lanes = self.quarter(i, 0, self.h, self.color, side)
        return self.arrs[i][0].at[rows, lanes]

    def part(self, i, m, flip_h=0, flip_c=0, side=None, d=None):
        src, out = self.arrs[i]
        d = DIST[m] if d is None else d
        base = ((self.p - d + 8) % 8) * src.shape[0]
        h = 1 - self.h if flip_h else self.h
        color = 1 - self.color if flip_c else self.color
        rows, lanes = self.quarter(i, base, h, color, side)
        return out.at[rows, lanes]

    def got(self, ref, sem):
        rcopy(ref, ref, sem, sem, self.partner).wait_recv()

    def direct(self):
        for m in (6, 4, 5, 2, 3, 0, 1):
            for i in range(2):
                d = DIST[m] if m < 6 else (4, -4)[i]
                dst = self.part(i, m, d=0)
                self.net.start(self.own(i), dst, self.zs.at[i, m], self.zr.at[i, m], self.at(d))

    def first(self, i):
        for di, d in enumerate((1, -1)):
            dst = self.part(i, di, d=0)
            self.net.start(self.own(i), dst, self.zs.at[i, di], self.zr.at[i, di], self.at(d))

    def spread(self, i, m):
        ref = self.part(i, m)
        self.net.start(ref, ref, self.ps.at[i, m], self.pr.at[i, m], self.partner)
        to = self.plane[m % 4]
        self.net.start(ref, ref, self.ns.at[i, m], self.nr.at[i, m], to)

    def take(self, i, m):
        self.got(self.part(i, m), self.zr.at[i, m])
        self.spread(i, m)

    def hop(self, i, t):
        for di, d in enumerate((1, -1)):
            m = (t - 1) * 2 + di
            self.got(self.part(i, m), self.zr.at[i, m])
            side = di if t == 3 else None
            ref = self.part(i, m, side=side)
            n = m + 2
            self.net.start(ref, ref, self.zs.at[i, n], self.zr.at[i, n], self.at(d))
            self.spread(i, m)

    def far(self, i):
        for di in range(2):
            self.got(self.part(i, 6, side=di), self.zr.at[i, 6 + di])
        self.spread(i, 6)

    def near(self, i):
        for m in range(7):
            ref = self.part(i, m, flip_c=1)
            self.got(ref, self.nr.at[i, m])
            self.net.start(ref, ref, self.ps.at[i, 7 + m], self.pr.at[i, 7 + m], self.partner)

    def done(self, i):
        for m in range(7):
            self.got(self.part(i, m, flip_h=1), self.pr.at[i, m])
        for m in range(7):
            self.got(self.part(i, m, flip_h=1, flip_c=1), self.pr.at[i, 7 + m])


class Gather:
    def __init__(self, net, kv, place, ss, rs, ps, pr):
        self.net, self.kv = net, kv
        c, p, zh, x, y, h = place
        self.ss, self.rs, self.ps, self.pr = ss, rs, ps, pr
        self.partner = (c + 1 - 2 * h, p)
        self.ap = (ctx_of(zh, (x + 1 - h) % 4, (y + h) % 4, h), p)
        self.am = (ctx_of(zh, (x + 3 + h) % 4, (y + 4 - h) % 4, h), p)
        self.bp = (ctx_of(zh, (x + h) % 4, (y + 1 - h) % 4, h), p)
        self.bm = (ctx_of(zh, (x + 4 - h) % 4, (y + 3 + h) % 4, h), p)

    def slot(self, g, j, m, r=0):
        return self.kv.at[((g * 4 + j) * 2 + r) * 4 + m]

    def half(self, g, j, m, k):
        return self.kv.at[((g * 4 + j) * 2) * 4 + m, pl.ds(k * HB, HB), :]

    def got(self, ref, k):
        rcopy(ref, ref, self.ss.at[k], self.rs.at[k], self.partner).wait_recv()

    def send(self, src, dst, k, dev):
        self.net.start(src, dst, self.ss.at[k], self.rs.at[k], dev)

    def to_b(self, g, j, src=None):
        src = self.slot(g, j, 0) if src is None else src
        k = 20 * g + 4 + 4 * j
        self.send(src, self.slot(g, j, 1), k, self.bp)
        self.send(src, self.slot(g, j, 2), k + 1, self.bm)

    def to_partner(self, g, j, m, src=None):
        src = self.slot(g, j, m) if src is None else src
        k = 16 * g + 4 * j + m
        self.net.start(src, self.slot(g, j, m, 1), self.ps.at[k], self.pr.at[k], self.partner)

    def own(self, g, src=None):
        a = self.slot(g, 0, 0) if src is None else src
        self.send(a, self.slot(g, 1, 0), 20 * g, self.ap)
        self.send(a, self.slot(g, 2, 0), 20 * g + 1, self.am)
        self.to_b(g, 0, src)
        self.to_partner(g, 0, 0, src)

    def a_near(self, g):
        for j, k, dev in ((1, 0, self.ap), (2, 1, self.am)):
            self.got(self.slot(g, j, 0), 20 * g + k)
            self.send(self.half(g, j, 0, k), self.half(g, 3, 0, k), 20 * g + 2 + k, dev)
            self.to_b(g, j)
            self.to_partner(g, j, 0)

    def a_far(self, g):
        for k in range(2):
            self.got(self.half(g, 3, 0, k), 20 * g + 2 + k)
        self.to_b(g, 3)
        self.to_partner(g, 3, 0)

    def b_near(self, g, j):
        base = 20 * g + 4 + 4 * j
        for m, k, dev in ((1, 0, self.bp), (2, 1, self.bm)):
            self.got(self.slot(g, j, m), base + k)
            self.send(self.half(g, j, m, k), self.half(g, j, 3, k), base + 2 + k, dev)
            self.to_partner(g, j, m)

    def b_far(self, g, j):
        base = 20 * g + 4 + 4 * j
        for k in range(2):
            self.got(self.half(g, j, 3, k), base + 2 + k)
        self.to_partner(g, j, 3)

    def from_partner(self, g, j):
        for m in range(4):
            k = 16 * g + 4 * j + m
            ref = self.slot(g, j, m, 1)
            rcopy(ref, ref, self.ps.at[k], self.pr.at[k], self.partner).wait_recv()


def front_kernel(
    tok_hbm, wk, wv, wq, wo, gain, wpair_hbm,
    seq, RB, CB,
    WK, WV, WQ, WO, tok, wpair, kv, blk, q, acc, high, mixed, rb, cb, HM, HL, HR,
    wzs, wzr, wns, wnr, wps, wpr, kss, krs, kps, kpr, zs, zr, ls, hello,
    rs_s, rs_r, z_s, z_r, y_s, y_r, els,
):
    place = coords()
    c, p, zh, x, y, h = place
    net = Net()
    arrs = ((wk, WK), (wv, WV), (wq, WQ), (wo, WO))
    ring = Weights(net, arrs, place, wzs, wzr, wns, wnr, wps, wpr)
    kvs = Gather(net, kv, place, kss, krs, kps, kpr)
    near = [ring.at(d) for d in (1, -1, 2, -2, 3, -3, 4, -4)]
    enter(near + ring.plane + [ring.partner])
    ring.direct()
    ring.first(2)
    pl.semaphore_signal(hello, inc=1, device_id=ring.at(-4), device_id_type=MESH)
    locs = []
    for i, (src, out) in enumerate(arrs):
        r = src.shape[0]
        locs.append((src, out.at[pl.ds(pl.multiple_of(p * r, r), r), :]))
    locs += [(tok_hbm, tok), (wpair_hbm, wpair)]
    locs = [pltpu.make_async_copy(src, dst, ls.at[i]) for i, (src, dst) in enumerate(locs)]
    for cp in locs:
        cp.start()

    for m in range(4):
        ring.take(0, m)
        ring.take(1, m)
    ring.hop(2, 1)
    for m in range(4, 7):
        ring.take(0, m)
        ring.take(1, m)
    ring.hop(2, 2)
    for i in (0, 1, 4):
        locs[i].wait()
    ring.near(0)
    ring.near(1)
    ring.done(0)
    ring.done(1)
    t = tok[...]
    blk[0:128, :] = jnp.dot(t, WK[...], preferred_element_type=F32).astype(BF)
    v = jnp.dot(t, WV[...], preferred_element_type=F32)
    blk[128:256, :] = v[:, :128].astype(BF)
    blk[256:320, :] = jnp.concatenate([v[0:64, 128:192], v[64:128, 128:192]], axis=1).astype(BF)

    pl.semaphore_wait(hello, 1)
    flip = (c + 32 - 64 * zh, p)
    net.start(blk, kvs.slot(1, 0, 0), zs, zr, flip)
    kvs.own(0, blk)
    loc = pltpu.make_async_copy(blk, kvs.slot(0, 0, 0), ls.at[6])
    loc.start()
    acc[...] = jnp.zeros_like(acc)
    high[...] = jnp.full_like(high, -1e30)
    ring.hop(2, 3)
    kvs.a_near(0)
    ring.far(2)
    kvs.b_near(0, 0)
    ring.near(2)
    ring.first(3)
    kvs.a_far(0)
    kvs.b_far(0, 0)
    kvs.b_near(0, 1)
    locs[2].wait()
    ring.done(2)
    qq = jnp.dot(tok[...], WQ[...], preferred_element_type=F32).astype(BF)
    for n in range(H):
        q[n * 128 : (n + 1) * 128, :] = qq[:, n * KEY : (n + 1) * KEY]
    loc.wait()

    scale = KEY ** (-0.5) * 1.4426950408889634

    def attend(g, j):
        kvs.from_partner(g, j)
        part = kv[pl.ds((g * 4 + j) * 8, 8)]
        k = part[:, 0:128, :].reshape(1024, 128)
        v1 = part[:, 128:256, :].reshape(1024, 128)
        lo = part[:, 256:320, :].astype(F32)
        hi = pltpu.roll(lo.reshape(512, 128), 64, 1).reshape(8, 64, 128)
        v2 = jnp.concatenate([lo, hi], axis=1).reshape(1024, 128)
        lane = lax.broadcasted_iota(jnp.int32, (1024, 128), 1)
        v2 = jnp.where(lane == 64, 1.0, v2).astype(BF)
        m = high[:, 0:1]
        s = lax.dot_general(q[...], k, (((1,), (1,)), ((), ())), preferred_element_type=F32)
        m2 = jnp.maximum(m, jnp.max(s, axis=1, keepdims=True))
        w = jnp.exp2((s - m2) * scale).astype(BF)
        o = jnp.dot(w, jnp.concatenate([v1, v2], axis=1), preferred_element_type=F32)
        acc[...] = acc[...] * jnp.exp2((m - m2) * scale) + o
        high[...] = jnp.broadcast_to(m2, high.shape)

    kvs.b_near(0, 2)
    attend(0, 0)
    kvs.b_near(0, 3)
    ring.hop(3, 1)
    for j in (1, 2, 3):
        kvs.b_far(0, j)
    attend(0, 1)
    other = kvs.slot(1, 0, 0)
    rcopy(other, other, zs, zr, flip).wait_recv()
    kvs.own(1)
    ring.hop(3, 2)
    attend(0, 2)
    kvs.a_near(1)
    kvs.b_near(1, 0)
    kvs.a_far(1)
    ring.hop(3, 3)
    attend(0, 3)
    kvs.b_far(1, 0)
    kvs.b_near(1, 1)
    kvs.b_near(1, 2)
    attend(1, 0)
    kvs.b_near(1, 3)
    ring.far(3)
    for j in (1, 2, 3):
        kvs.b_far(1, j)
    ring.near(3)
    for j in (1, 2, 3):
        attend(1, j)
    locs[3].wait()
    locs[5].wait()
    ring.done(3)

    a = acc[...]
    mx = (a[:, 0:VAL] / a[:, VAL : VAL + 1]).astype(BF)
    for n in range(H):
        mixed[:, n * VAL : (n + 1) * VAL] = mx[n * 128 : (n + 1) * 128, :]
    summed = tok[...].astype(F32) + jnp.dot(mixed[...], WO[...], preferred_element_type=F32)
    seq[...] = summed.astype(BF)
    pooled = jnp.mean(summed.reshape(8, POOL, summed.shape[1]), axis=1)
    ms = jnp.mean(pooled * pooled, axis=-1, keepdims=True)
    normed = (pooled * lax.rsqrt(ms + 1e-06) * gain[...].reshape(1, -1)).astype(BF)
    both = jnp.dot(normed, wpair[...], preferred_element_type=F32).astype(BF)
    rb[...] = both[:, :PC]
    cb[...] = both[:, PC:]
    exchange(rb, cb, RB, CB, HM, HL, HR, rs_s, rs_r, z_s, z_r, y_s, y_r, els)
    net.finish()


def front(tok, wk, wv, wq, wo, gain, wpair):
    vm = pl.BlockSpec(memory_space=pltpu.VMEM)
    dma = pltpu.SemaphoreType.DMA
    hold = pltpu.VMEM((8, 8, PC), BF)
    hbm = pl.BlockSpec(memory_space=pl.ANY)
    return pl.pallas_call(
        front_kernel,
        out_shape=(
            jax.ShapeDtypeStruct(tok.shape, BF),
            jax.ShapeDtypeStruct((3, 8, 8, PC), BF),
            jax.ShapeDtypeStruct((10, 8, 8, PC), BF),
        ),
        in_specs=[hbm] * 5 + [vm, hbm],
        out_specs=(vm,) * 3,
        scratch_shapes=[pltpu.VMEM((8 * w.shape[0], w.shape[1]), BF) for w in (wk, wv, wq, wo)]
        + [
            pltpu.VMEM(tok.shape, BF),
            pltpu.VMEM(wpair.shape, BF),
            pltpu.VMEM((64, BR, 128), BF),
            pltpu.VMEM((BR, 128), BF),
            pltpu.VMEM((512, 128), BF),
            pltpu.VMEM((512, 256), F32),
            pltpu.VMEM((512, 128), F32),
            pltpu.VMEM((128, H * VAL), BF),
            pltpu.VMEM((8, PC), BF),
            pltpu.VMEM((8, PC), BF),
            hold,
            hold,
            hold,
        ]
        + [dma((4, 8)), dma((4, 8)), dma((4, 7)), dma((4, 7)), dma((4, 14)), dma((4, 14))]
        + [dma((40,)), dma((40,)), dma((32,)), dma((32,)), dma, dma, dma((7,))]
        + [pltpu.SemaphoreType.REGULAR]
        + [dma((3, 8)), dma((3, 8)), dma((3, 8)), dma((3, 8)), dma((3, 7)), dma((10,)), dma((7,))],
        compiler_params=pltpu.CompilerParams(
            collective_id=0, has_side_effects=True, vmem_limit_bytes=VMEM_LIMIT
        ),
        name="front",
    )(tok, wk, wv, wq, wo, gain, wpair)


def conv_kernel(rb, cb, w, seq_in, out, seq_out, tile, line, sems):
    bring = pltpu.make_async_copy(seq_in, line, sems.at[8])
    bring.start()

    def put(s):
        return pltpu.make_async_copy(tile.at[s], out.at[s], sems.at[s])

    def seq(s, carry):
        prev = rb[0, pl.ds(s, 1)].reshape(8, PC).astype(F32)
        own = rb[1, pl.ds(s, 1)].reshape(8, PC).astype(F32)
        nxt = rb[2, pl.ds(s, 1)].reshape(8, PC).astype(F32)
        col = jnp.concatenate([cb[k, pl.ds(s, 1)].reshape(8, PC) for k in range(10)], axis=0).astype(F32)
        rows = [prev[6:7], prev[7:8]] + [own[k : k + 1] for k in range(8)] + [nxt[0:1], nxt[1:2]]
        shifted = [col[6 + 2 * b : 70 + 2 * b] for b in range(3)]
        maps = [jnp.concatenate([(r * cs).astype(BF) for r in rows], axis=0) for cs in shifted]
        lhs = jnp.concatenate(
            [maps[b][128 * a : 128 * a + 512] for a in range(3) for b in range(3)], axis=1
        )
        t = jnp.dot(lhs, w[...], preferred_element_type=F32)
        res = maps[1][128:640].astype(F32) + jax.nn.gelu(t)
        tile[pl.ds(s, 1)] = res.astype(BF).reshape(1, 8, 64, PC)
        put(s).start()
        return carry

    lax.fori_loop(0, 8, seq, 0)
    bring.wait()
    give = pltpu.make_async_copy(line, seq_out, sems.at[8])
    give.start()
    for s in range(8):
        put(s).wait()
    give.wait()


def convolve(rb, cb, w, seq):
    vm = pl.BlockSpec(memory_space=pltpu.VMEM)
    hbm = pl.BlockSpec(memory_space=pl.ANY)
    return pl.pallas_call(
        conv_kernel,
        out_shape=(jax.ShapeDtypeStruct((8, 8, 64, PC), BF), jax.ShapeDtypeStruct(seq.shape, BF)),
        in_specs=[vm] * 3 + [hbm],
        out_specs=(hbm, hbm),
        scratch_shapes=[
            pltpu.VMEM((8, 8, 64, PC), BF),
            pltpu.VMEM(seq.shape, BF),
            pltpu.SemaphoreType.DMA((9,)),
        ],
        compiler_params=pltpu.CompilerParams(vmem_limit_bytes=VMEM_LIMIT),
        name="convolve",
    )(rb, cb, w, seq)


def on_device(tokens, w_query, w_key, w_value, w_out, norm_gain, w_pair, conv_weight):
    tok = tokens.reshape(tokens.shape[1], tokens.shape[2])
    seq, rb, cb = front(tok, w_key, w_value, w_query, w_out, norm_gain, w_pair)
    out, seq = convolve(rb, cb, conv_weight.reshape(9 * PC, PC), seq)
    return seq.reshape(tokens.shape), out


def solution(mesh):
    return jax.shard_map(
        on_device,
        mesh=mesh,
        in_specs=(
            P("pair", "ctx", None),
            P("pair", None),
            P("pair", None),
            P("pair", None),
            P("pair", None),
            P(),
            P(),
            P(),
        ),
        out_specs=(P("pair", "ctx", None), P(None, "ctx", "pair", None)),
        check_vma=False,
    )
```

```python
import functools

import jax
import jax.numpy as jnp
from jax import lax
from jax.experimental import pallas as pl
from jax.experimental.pallas import tpu as pltpu
from jax.sharding import PartitionSpec as P

H = 4
KEY = 128
VAL = 192
PC = 128
POOL = 16
MESH = pl.DeviceIdType.MESH
BF = jnp.bfloat16
F32 = jnp.float32
BR = 320
HB = BR // 2
VMEM_LIMIT = 60 * 1024 * 1024


def coords():
    c = lax.axis_index("ctx")
    p = lax.axis_index("pair")
    return c, p, c // 32, (c // 8) % 4, (c // 2) % 4, c % 2


def ctx_of(zh, x, y, core):
    return ((zh * 4 + x) * 4 + y) * 2 + core


def at_z(c, zh, p, d):
    z = (zh * 8 + p + d + 16) % 16
    return ((z // 8) * 32 + c % 32, z % 8)


def rcopy(src, dst, ssem, rsem, dev):
    return pltpu.make_async_remote_copy(
        src_ref=src, dst_ref=dst, send_sem=ssem, recv_sem=rsem, device_id=dev, device_id_type=MESH
    )


def enter(devs):
    barrier = pltpu.get_barrier_semaphore()
    for dev in devs:
        pl.semaphore_signal(barrier, inc=1, device_id=dev, device_id_type=MESH)
    pl.semaphore_wait(barrier, len(devs))


def exchange(rb, cb, RB, CB, HM, HL, HR, rs_s, rs_r, z_s, z_r, y_s, y_r):
    c, p, zh, x, y, h = coords()
    cn, cv = (c + 1) % 64, (c + 63) % 64
    pp = [(p + k) % 8 for k in range(8)]
    yc = []
    for k in range(4):
        for e in range(2):
            if k or e:
                yc.append((ctx_of(zh, x, (y + k) % 4, (h + e) % 2), p))

    def cond(pred, fn):
        if pred is None:
            fn()
        else:
            pl.when(pred)(fn)

    tgt = c // 8
    jobs = [
        (tgt, HM, 0, None),
        (tgt + 1, HL, 1, (c % 8 == 7) & (tgt < 7)),
        (tgt - 1, HR, 2, (c % 8 == 0) & (tgt > 0)),
    ]

    for t, buf, b, pred in jobs:
        for f in (1, 0):
            for k in (2, 1, 3, 0):
                dc = ctx_of(zh if f == 0 else 1 - zh, (x + k) % 4, y, h)

                def go(t=t, buf=buf, b=b, dc=dc):
                    send(cb, buf.at[p], z_s.at[b], z_r.at[b], (dc, t))

                if f or k:
                    cond(pred, go)
                else:
                    away = t != p
                    cond(away if pred is None else away & pred, go)

    for b, dc, pred in ((0, cn, c < 63), (2, cv, c > 0)):

        @pl.when(pred)
        def _():
            for k in range(8):
                send(rb, RB.at[b, p], rs_s.at[b], rs_r.at[b], (dc, pp[k]))

    for k in range(1, 8):
        send(rb, RB.at[1, p], rs_s.at[1], rs_r.at[1], (c, pp[k]))
    RB[1, pl.ds(p, 1)] = rb[...].reshape(1, 8, PC)
    for t, buf, b, pred in jobs:

        @pl.when((t == p) if pred is None else (t == p) & pred)
        def _():
            buf[pl.ds(p, 1)] = cb[...].reshape(1, 8, PC)

    @pl.when(c == 0)
    def _():
        RB[0] = jnp.zeros((8, 8, PC), BF)

    @pl.when(c == 63)
    def _():
        RB[2] = jnp.zeros((8, 8, PC), BF)

    @pl.when(p == 0)
    def _():
        CB[0] = jnp.zeros((8, 8, PC), BF)

    @pl.when(p == 7)
    def _():
        CB[9] = jnp.zeros((8, 8, PC), BF)

    mine = 1 + 2 * y + h
    spreads = (
        (HM, 0, p, None, mine),
        (HL, 1, p - 1, (y == 3) & (h == 1) & (p > 0), 0),
        (HR, 2, p + 1, (y == 0) & (h == 0) & (p < 7), 9),
    )
    for buf, b, owner, member, cslot in spreads:

        def take(buf=buf, b=b, owner=owner, cslot=cslot):
            inside = (zh == owner // 4) & (x == owner % 4)
            pl.when(inside)(lambda: received(buf.at[pl.ds(0, 7)], z_r.at[b]))
            pl.when(jnp.logical_not(inside))(lambda: received(buf, z_r.at[b]))
            for k in range(7):
                send(buf, CB.at[cslot], y_s.at[b], y_r.at[b], yc[k])
            CB[pl.ds(cslot, 1)] = buf[...].reshape(1, 8, 8, PC)

        cond(member, take)

    received(CB.at[pl.ds(1, 7)], y_r.at[0])

    @pl.when((p > 0) & jnp.logical_not((y == 3) & (h == 1)))
    def _():
        received(CB.at[0], y_r.at[1])

    @pl.when((p < 7) & jnp.logical_not((y == 0) & (h == 0)))
    def _():
        received(CB.at[9], y_r.at[2])

    received(RB.at[1, pl.ds(0, 7)], rs_r.at[1])
    drained(RB.at[1, pl.ds(0, 7)], rs_s.at[1])
    for b, came, went in ((0, c > 0, c < 63), (2, c < 63, c > 0)):
        pl.when(came)(lambda b=b: received(RB.at[b], rs_r.at[b]))
        pl.when(went)(lambda b=b: drained(RB.at[b], rs_s.at[b]))
    for t, buf, b, pred in jobs:

        def gone(t=t, buf=buf, b=b):
            pl.when(t == p)(lambda: drained(buf.at[pl.ds(0, 7)], z_s.at[b]))
            pl.when(t != p)(lambda: drained(buf, z_s.at[b]))

        cond(pred, gone)
    for buf, b, owner, member, cslot in spreads:
        cond(member, lambda b=b: drained(CB.at[pl.ds(0, 7)], y_s.at[b]))


def send(src, dst, s, r, dev):
    rcopy(src, dst, s, r, dev).start()


def received(ref, sem):
    rcopy(ref, ref, sem, sem, (0, 0)).wait_recv()


def drained(ref, sem):
    rcopy(ref, ref, sem, sem, (0, 0)).wait_send()


DIST = (1, -1, 2, -2, 3, -3, 4)


class Weights:
    def __init__(self, arrs, place, ss, zr, nr, pr):
        self.arrs = arrs
        self.c, self.p, self.zh, x, y, self.h = place
        self.color = (x + y) % 2
        self.partner = (self.c + 1 - 2 * self.h, self.p)
        self.plane = [
            (ctx_of(self.zh, (x + dx) % 4, (y + dy) % 4, self.h), self.p)
            for dx, dy in ((1, 0), (3, 0), (0, 1), (0, 3))
        ]
        self.ss, self.zr, self.nr, self.pr = ss, zr, nr, pr

    def at(self, d):
        return at_z(self.c, self.zh, self.p, d)

    def quarter(self, i, base, h, color, side=None):
        src, _ = self.arrs[i]
        r, w = src.shape
        if i < 3:
            n = r // 4
            row, lane, wide = base + h * 2 * n + color * n, 0, w
        else:
            n = r // 2
            row, lane, wide = base + h * n, pl.multiple_of(color * (w // 2), w // 2), w // 2
        if side is not None:
            wide = wide // 2
            lane = lane + side * wide
            if i == 3:
                lane = pl.multiple_of(lane, wide)
        return pl.ds(pl.multiple_of(row, n), n), pl.ds(lane, wide)

    def own(self, i, side=None):
        rows, lanes = self.quarter(i, 0, self.h, self.color, side)
        return self.arrs[i][0].at[rows, lanes]

    def part(self, i, m, flip_h=0, flip_c=0, side=None, d=None):
        src, out = self.arrs[i]
        d = DIST[m] if d is None else d
        base = ((self.p - d + 8) % 8) * src.shape[0]
        h = 1 - self.h if flip_h else self.h
        color = 1 - self.color if flip_c else self.color
        rows, lanes = self.quarter(i, base, h, color, side)
        return out.at[rows, lanes]

    def first(self, i):
        for di, d in enumerate((1, -1)):
            dst = self.part(i, di, d=0)
            send(self.own(i), dst, self.ss.at[i], self.zr.at[i, di], self.at(d))

    def hop(self, i, t):
        for di, d in enumerate((1, -1)):
            m = (t - 1) * 2 + di
            received(self.part(i, m), self.zr.at[i, m])
            if t < 3 or i >= 2 or i == di:
                ref = self.part(i, m, side=di if t == 3 and i >= 2 else None)
                send(ref, ref, self.ss.at[i], self.zr.at[i, min(m + 2, 6)], self.at(d))
            self.spread(i, m)

    def spread(self, i, m):
        ref = self.part(i, m)
        send(ref, ref, self.ss.at[i], self.pr.at[i], self.partner)
        to = self.plane[m % 4]
        send(ref, ref, self.ss.at[i], self.nr.at[i, m], to)

    def take(self, i, m):
        received(self.part(i, m), self.zr.at[i, m])
        self.spread(i, m)

    def near(self, i):
        for m in range(7):
            ref = self.part(i, m, flip_c=1)
            received(ref, self.nr.at[i, m])
            send(ref, ref, self.ss.at[i], self.pr.at[i], self.partner)

    def done(self, i):
        src, out = self.arrs[i]
        received(out.at[pl.ds(0, 7 * src.shape[0] // 2), :], self.pr.at[i])

    def finish(self):
        for i, (src, out) in enumerate(self.arrs):
            drained(out.at[pl.ds(0, 7 * src.shape[0]), :], self.ss.at[i])


class Gather:
    def __init__(self, kv, place, ss, rs, pr):
        self.kv = kv
        c, p, zh, x, y, h = place
        self.ss, self.rs, self.pr = ss, rs, pr
        self.partner = (c + 1 - 2 * h, p)
        self.ap = (ctx_of(zh, (x + 1 - h) % 4, (y + h) % 4, h), p)
        self.am = (ctx_of(zh, (x + 3 + h) % 4, (y + 4 - h) % 4, h), p)
        self.af = (ctx_of(zh, (x + 2 - 2 * h) % 4, (y + 2 * h) % 4, h), p)
        self.bp = (ctx_of(zh, (x + h) % 4, (y + 1 - h) % 4, h), p)
        self.bm = (ctx_of(zh, (x + 4 - h) % 4, (y + 3 + h) % 4, h), p)

    def slot(self, g, j, m, r=0):
        return self.kv.at[((g * 4 + j) * 2 + r) * 4 + m]

    def half(self, g, j, m, k):
        return self.kv.at[((g * 4 + j) * 2) * 4 + m, pl.ds(k * HB, HB), :]

    def got(self, ref, k):
        received(ref, self.rs.at[k])

    def send(self, src, dst, k, dev):
        send(src, dst, self.ss, self.rs.at[k], dev)

    def to_b(self, g, j, src=None):
        src = self.slot(g, j, 0) if src is None else src
        k = 15 * g + 3 + 3 * j
        self.send(src, self.slot(g, j, 1), k, self.bp)
        self.send(src, self.slot(g, j, 2), k + 1, self.bm)

    def to_partner(self, g, j, m, src=None):
        src = self.slot(g, j, m) if src is None else src
        send(src, self.slot(g, j, m, 1), self.ss, self.pr.at[4 * g + j], self.partner)

    def own(self, g, src=None):
        a = self.slot(g, 0, 0) if src is None else src
        self.send(a, self.slot(g, 1, 0), 15 * g, self.ap)
        self.send(a, self.slot(g, 2, 0), 15 * g + 1, self.am)
        self.send(a, self.slot(g, 3, 0), 15 * g + 2, self.af)
        self.to_b(g, 0, src)
        self.to_partner(g, 0, 0, src)

    def a_near(self, g):
        for j, k in ((1, 0), (2, 1)):
            self.got(self.slot(g, j, 0), 15 * g + k)
            self.to_b(g, j)
            self.to_partner(g, j, 0)

    def a_far(self, g):
        self.got(self.slot(g, 3, 0), 15 * g + 2)
        self.to_b(g, 3)
        self.to_partner(g, 3, 0)

    def b_near(self, g, j):
        base = 15 * g + 3 + 3 * j
        for m, k, dev in ((1, 0, self.bp), (2, 1, self.bm)):
            self.got(self.slot(g, j, m), base + k)
            self.send(self.half(g, j, m, k), self.half(g, j, 3, k), base + 2, dev)
            self.to_partner(g, j, m)

    def b_far(self, g, j):
        self.got(self.slot(g, j, 3), 15 * g + 3 + 3 * j + 2)
        self.to_partner(g, j, 3)

    def from_partner(self, g, j):
        received(self.kv.at[pl.ds(((g * 4 + j) * 2 + 1) * 4, 4)], self.pr.at[4 * g + j])

    def finish(self):
        drained(self.kv, self.ss)


def front_kernel(
    tok_hbm, wk, wv, wq, wo, gain, wpair_hbm,
    seq, RB, CB,
    WK, WV, WQ, WO, tok, wpair, kv, blk, relay, q, acc, high, mixed, rb, cb, HM, HL, HR,
    wss, wzr, wnr, wpr, kss, krs, kpr, zr, hr, ls, rs_s, rs_r, z_s, z_r, y_s, y_r,
):
    place = coords()
    c, p, zh, x, y, h = place
    arrs = ((wk, WK), (wv, WV), (wq, WQ), (wo, WO))
    ring = Weights(arrs, place, wss, wzr, wnr, wpr)
    kvs = Gather(kv, place, kss, krs, kpr)
    enter([ring.at(1), ring.at(-1), ring.partner] + ring.plane)
    for i in range(3):
        ring.first(i)
    locs = []
    for i, (src, out) in enumerate(arrs):
        r = src.shape[0]
        locs.append((src, out.at[pl.ds(pl.multiple_of(p * r, r), r), :]))
    locs += [(tok_hbm, tok), (wpair_hbm, wpair)]
    locs = [pltpu.make_async_copy(src, dst, ls.at[i]) for i, (src, dst) in enumerate(locs)]
    for cp in locs:
        cp.start()

    for n in (1, 2, 3):
        for i in range(3):
            ring.hop(i, n)
    ring.take(0, 6)
    ring.take(1, 6)
    for i in (0, 1, 4):
        locs[i].wait()
    ring.near(0)
    ring.near(1)
    ring.take(2, 6)
    ring.done(0)
    ring.done(1)
    t = tok[...]
    blk[0:128, :] = jnp.dot(t, WK[...], preferred_element_type=F32).astype(BF)
    v = jnp.dot(t, WV[...], preferred_element_type=F32)
    blk[128:256, :] = v[:, :128].astype(BF)
    blk[256:320, :] = jnp.concatenate([v[0:64, 128:192], v[64:128, 128:192]], axis=1).astype(BF)

    for k in range(2):
        send(blk.at[pl.ds(k * HB, HB), :], relay.at[k], kss, hr.at[k], ring.at((4, -4)[k]))
    kvs.own(0, blk)
    loc = pltpu.make_async_copy(blk, kvs.slot(0, 0, 0), ls.at[6])
    loc.start()
    acc[...] = jnp.zeros_like(acc)
    high[...] = jnp.full_like(high, -1e30)
    kvs.a_near(0)
    kvs.a_far(0)
    ring.near(2)
    kvs.b_near(0, 0)
    for k in range(2):
        received(relay.at[k], hr.at[k])
        send(relay.at[k], kvs.half(1, 0, 0, k), kss, zr, ring.at((4, -4)[k]))
    ring.first(3)
    kvs.b_near(0, 1)
    kvs.b_near(0, 2)
    kvs.b_far(0, 0)
    kvs.b_near(0, 3)
    loc.wait()
    locs[2].wait()
    ring.done(2)
    qq = jnp.dot(tok[...], WQ[...], preferred_element_type=F32).astype(BF)
    for n in range(H):
        q[n * 128 : (n + 1) * 128, :] = qq[:, n * KEY : (n + 1) * KEY]
    ring.hop(3, 1)
    for j in (1, 2, 3):
        kvs.b_far(0, j)
    received(kvs.slot(1, 0, 0), zr)
    kvs.own(1)

    scale = KEY ** (-0.5) * 1.4426950408889634

    def attend(g, j):
        kvs.from_partner(g, j)
        part = kv[pl.ds((g * 4 + j) * 8, 8)]
        k = part[:, 0:128, :].reshape(1024, 128)
        v1 = part[:, 128:256, :].reshape(1024, 128)
        lo = part[:, 256:320, :].astype(F32)
        hi = pltpu.roll(lo.reshape(512, 128), 64, 1).reshape(8, 64, 128)
        v2 = jnp.concatenate([lo, hi], axis=1).reshape(1024, 128)
        lane = lax.broadcasted_iota(jnp.int32, (1024, 128), 1)
        v2 = jnp.where(lane == 64, 1.0, v2).astype(BF)
        m = high[:, 0:1]
        s = lax.dot_general(q[...], k, (((1,), (1,)), ((), ())), preferred_element_type=F32)
        m2 = jnp.maximum(m, jnp.max(s, axis=1, keepdims=True))
        w = jnp.exp2((s - m2) * scale).astype(BF)
        o = jnp.dot(w, jnp.concatenate([v1, v2], axis=1), preferred_element_type=F32)
        acc[...] = acc[...] * jnp.exp2((m - m2) * scale) + o
        high[...] = jnp.broadcast_to(m2, high.shape)

    attend(0, 0)
    ring.hop(3, 2)
    kvs.a_near(1)
    kvs.a_far(1)
    kvs.b_near(1, 0)
    attend(0, 1)
    ring.hop(3, 3)
    kvs.b_near(1, 1)
    kvs.b_near(1, 2)
    kvs.b_far(1, 0)
    attend(0, 2)
    ring.take(3, 6)
    kvs.b_near(1, 3)
    kvs.b_far(1, 1)
    kvs.b_far(1, 2)
    attend(0, 3)
    ring.near(3)
    kvs.b_far(1, 3)
    for j in range(4):
        attend(1, j)
    locs[3].wait()
    locs[5].wait()
    ring.done(3)

    a = acc[...]
    mx = (a[:, 0:VAL] / a[:, VAL : VAL + 1]).astype(BF)
    for n in range(H):
        mixed[:, n * VAL : (n + 1) * VAL] = mx[n * 128 : (n + 1) * 128, :]
    summed = tok[...].astype(F32) + jnp.dot(mixed[...], WO[...], preferred_element_type=F32)
    seq[...] = summed.astype(BF)
    pooled = jnp.mean(summed.reshape(8, POOL, summed.shape[1]), axis=1)
    ms = jnp.mean(pooled * pooled, axis=-1, keepdims=True)
    normed = (pooled * lax.rsqrt(ms + 1e-06) * gain[...].reshape(1, -1)).astype(BF)
    both = jnp.dot(normed, wpair[...], preferred_element_type=F32).astype(BF)
    rb[...] = both[:, :PC]
    cb[...] = both[:, PC:]
    exchange(rb, cb, RB, CB, HM, HL, HR, rs_s, rs_r, z_s, z_r, y_s, y_r)
    ring.finish()
    kvs.finish()


def front(tok, wk, wv, wq, wo, gain, wpair):
    vm = pl.BlockSpec(memory_space=pltpu.VMEM)
    dma = pltpu.SemaphoreType.DMA
    hold = pltpu.VMEM((8, 8, PC), BF)
    hbm = pl.BlockSpec(memory_space=pl.ANY)
    return pl.pallas_call(
        front_kernel,
        out_shape=(
            jax.ShapeDtypeStruct(tok.shape, BF),
            jax.ShapeDtypeStruct((3, 8, 8, PC), BF),
            jax.ShapeDtypeStruct((10, 8, 8, PC), BF),
        ),
        in_specs=[hbm] * 5 + [vm, hbm],
        out_specs=(vm,) * 3,
        scratch_shapes=[pltpu.VMEM((8 * w.shape[0], w.shape[1]), BF) for w in (wk, wv, wq, wo)]
        + [
            pltpu.VMEM(tok.shape, BF),
            pltpu.VMEM(wpair.shape, BF),
            pltpu.VMEM((64, BR, 128), BF),
            pltpu.VMEM((BR, 128), BF),
            pltpu.VMEM((2, HB, 128), BF),
            pltpu.VMEM((512, 128), BF),
            pltpu.VMEM((512, 256), F32),
            pltpu.VMEM((512, 128), F32),
            pltpu.VMEM((128, H * VAL), BF),
            pltpu.VMEM((8, PC), BF),
            pltpu.VMEM((8, PC), BF),
            hold,
            hold,
            hold,
        ]
        + [dma((4,)), dma((4, 7)), dma((4, 7)), dma((4,)), dma, dma((30,)), dma((8,)), dma, dma((2,)), dma((7,))]
        + [dma((3,))] * 6,
        compiler_params=pltpu.CompilerParams(
            collective_id=0, has_side_effects=True, vmem_limit_bytes=VMEM_LIMIT
        ),
        name="front",
    )(tok, wk, wv, wq, wo, gain, wpair)


def conv_kernel(rb, cb, w, seq_in, out, seq_out, tile, line, wide, sems):
    bring = pltpu.make_async_copy(seq_in, line, sems.at[8])
    bring.start()

    for r in range(4):
        for n in range(2):
            a = r - n
            for b in range(3):
                k = (3 * r + b) * PC
                if 0 <= a < 3:
                    tap = (3 * a + b) * PC
                    wide[k : k + PC, n * PC : (n + 1) * PC] = w[tap : tap + PC, :]
                else:
                    wide[k : k + PC, n * PC : (n + 1) * PC] = jnp.zeros((PC, PC), BF)

    def put(s):
        return pltpu.make_async_copy(tile.at[s], out.at[s], sems.at[s])

    first = (0, 4, 1, 5)

    def seq(s):
        prev = rb[0, pl.ds(s, 1)].reshape(8, PC).astype(F32)
        own = rb[1, pl.ds(s, 1)].reshape(8, PC).astype(F32)
        nxt = rb[2, pl.ds(s, 1)].reshape(8, PC).astype(F32)
        col = jnp.concatenate([cb[k, pl.ds(s, 1)].reshape(8, PC) for k in range(10)], axis=0).astype(F32)
        rows = [prev[6:7], prev[7:8]] + [own[k : k + 1] for k in range(8)] + [nxt[0:1], nxt[1:2]]
        shifted = [col[6 + 2 * b : 70 + 2 * b] for b in range(3)]
        maps = [[(r * cs).astype(BF) for r in rows] for cs in shifted]
        lhs = jnp.concatenate(
            [
                jnp.concatenate([maps[b][i + 2 * r] for i in first], axis=0)
                for r in range(4)
                for b in range(3)
            ],
            axis=1,
        )
        t = jnp.dot(lhs, wide[...], preferred_element_type=F32)
        for q, i in enumerate(first):
            for n in range(2):
                conv = t[64 * q : 64 * q + 64, n * PC : (n + 1) * PC]
                res = maps[1][i + 2 * n + 2].astype(F32) + jax.nn.gelu(conv)
                tile[pl.ds(s, 1), i + 2 * n] = res.astype(BF).reshape(1, 64, PC)
        put(s).start()

    def two(n, carry):
        seq(2 * n)
        seq(2 * n + 1)
        return carry

    lax.fori_loop(0, 4, two, 0)
    bring.wait()
    give = pltpu.make_async_copy(line, seq_out, sems.at[8])
    give.start()
    for s in range(8):
        put(s).wait()
    give.wait()


def convolve(rb, cb, w, seq):
    vm = pl.BlockSpec(memory_space=pltpu.VMEM)
    hbm = pl.BlockSpec(memory_space=pl.ANY)
    return pl.pallas_call(
        conv_kernel,
        out_shape=(jax.ShapeDtypeStruct((8, 8, 64, PC), BF), jax.ShapeDtypeStruct(seq.shape, BF)),
        in_specs=[vm] * 3 + [hbm],
        out_specs=(hbm, hbm),
        scratch_shapes=[
            pltpu.VMEM((8, 8, 64, PC), BF),
            pltpu.VMEM(seq.shape, BF),
            pltpu.VMEM((12 * PC, 2 * PC), BF),
            pltpu.SemaphoreType.DMA((9,)),
        ],
        compiler_params=pltpu.CompilerParams(vmem_limit_bytes=VMEM_LIMIT),
        name="convolve",
    )(rb, cb, w, seq)


def on_device(tokens, w_query, w_key, w_value, w_out, norm_gain, w_pair, conv_weight):
    tok = tokens.reshape(tokens.shape[1], tokens.shape[2])
    seq, rb, cb = front(tok, w_key, w_value, w_query, w_out, norm_gain, w_pair)
    out, seq = convolve(rb, cb, conv_weight.reshape(9 * PC, PC), seq)
    return seq.reshape(tokens.shape), out


def solution(mesh):
    return jax.shard_map(
        on_device,
        mesh=mesh,
        in_specs=(
            P("pair", "ctx", None),
            P("pair", None),
            P("pair", None),
            P("pair", None),
            P("pair", None),
            P(),
            P(),
            P(),
        ),
        out_specs=(P("pair", "ctx", None), P(None, "ctx", "pair", None)),
        check_vma=False,
    )
```

```python
import functools

import jax
import jax.numpy as jnp
from jax import lax
from jax.experimental import pallas as pl
from jax.experimental.pallas import tpu as pltpu
from jax.sharding import PartitionSpec as P

H = 4
KEY = 128
VAL = 192
PC = 128
POOL = 16
MESH = pl.DeviceIdType.MESH
BF = jnp.bfloat16
F32 = jnp.float32
BR = 320
HB = BR // 2
VMEM_LIMIT = 60 * 1024 * 1024


def coords():
    c = lax.axis_index("ctx")
    p = lax.axis_index("pair")
    return c, p, c // 32, (c // 8) % 4, (c // 2) % 4, c % 2


def ctx_of(zh, x, y, core):
    return ((zh * 4 + x) * 4 + y) * 2 + core


def at_z(c, zh, p, d):
    z = (zh * 8 + p + d + 16) % 16
    return ((z // 8) * 32 + c % 32, z % 8)


def rcopy(src, dst, ssem, rsem, dev):
    return pltpu.make_async_remote_copy(
        src_ref=src, dst_ref=dst, send_sem=ssem, recv_sem=rsem, device_id=dev, device_id_type=MESH
    )


def enter(devs):
    barrier = pltpu.get_barrier_semaphore()
    for dev in devs:
        pl.semaphore_signal(barrier, inc=1, device_id=dev, device_id_type=MESH)
    pl.semaphore_wait(barrier, len(devs))


def exchange(rb, cb, RB, CB, HM, HL, HR, rs_s, rs_r, z_s, z_r, y_s, y_r):
    c, p, zh, x, y, h = coords()
    cn, cv = (c + 1) % 64, (c + 63) % 64
    pp = [(p + k) % 8 for k in range(8)]
    yc = []
    for k in range(4):
        for e in range(2):
            if k or e:
                yc.append((ctx_of(zh, x, (y + k) % 4, (h + e) % 2), p))

    def cond(pred, fn):
        if pred is None:
            fn()
        else:
            pl.when(pred)(fn)

    tgt = c // 8
    jobs = [
        (tgt, HM, 0, None),
        (tgt + 1, HL, 1, (c % 8 == 7) & (tgt < 7)),
        (tgt - 1, HR, 2, (c % 8 == 0) & (tgt > 0)),
    ]

    for t, buf, b, pred in jobs:
        for f in (1, 0):
            for k in (2, 1, 3, 0):
                dc = ctx_of(zh if f == 0 else 1 - zh, (x + k) % 4, y, h)

                def go(t=t, buf=buf, b=b, dc=dc):
                    send(cb, buf.at[p], z_s.at[b], z_r.at[b], (dc, t))

                if f or k:
                    cond(pred, go)
                else:
                    away = t != p
                    cond(away if pred is None else away & pred, go)

    for b, dc, pred in ((0, cn, c < 63), (2, cv, c > 0)):

        @pl.when(pred)
        def _():
            for k in range(8):
                send(rb, RB.at[b, p], rs_s.at[b], rs_r.at[b], (dc, pp[k]))

    for k in range(1, 8):
        send(rb, RB.at[1, p], rs_s.at[1], rs_r.at[1], (c, pp[k]))
    RB[1, pl.ds(p, 1)] = rb[...].reshape(1, 8, PC)
    for t, buf, b, pred in jobs:

        @pl.when((t == p) if pred is None else (t == p) & pred)
        def _():
            buf[pl.ds(p, 1)] = cb[...].reshape(1, 8, PC)

    @pl.when(c == 0)
    def _():
        RB[0] = jnp.zeros((8, 8, PC), BF)

    @pl.when(c == 63)
    def _():
        RB[2] = jnp.zeros((8, 8, PC), BF)

    @pl.when(p == 0)
    def _():
        CB[0] = jnp.zeros((8, 8, PC), BF)

    @pl.when(p == 7)
    def _():
        CB[9] = jnp.zeros((8, 8, PC), BF)

    mine = 1 + 2 * y + h
    spreads = (
        (HM, 0, p, None, mine),
        (HL, 1, p - 1, (y == 3) & (h == 1) & (p > 0), 0),
        (HR, 2, p + 1, (y == 0) & (h == 0) & (p < 7), 9),
    )
    for buf, b, owner, member, cslot in spreads:

        def take(buf=buf, b=b, owner=owner, cslot=cslot):
            inside = (zh == owner // 4) & (x == owner % 4)
            pl.when(inside)(lambda: received(buf.at[pl.ds(0, 7)], z_r.at[b]))
            pl.when(jnp.logical_not(inside))(lambda: received(buf, z_r.at[b]))
            for k in range(7):
                send(buf, CB.at[cslot], y_s.at[b], y_r.at[b], yc[k])
            CB[pl.ds(cslot, 1)] = buf[...].reshape(1, 8, 8, PC)

        cond(member, take)

    received(CB.at[pl.ds(1, 7)], y_r.at[0])

    @pl.when((p > 0) & jnp.logical_not((y == 3) & (h == 1)))
    def _():
        received(CB.at[0], y_r.at[1])

    @pl.when((p < 7) & jnp.logical_not((y == 0) & (h == 0)))
    def _():
        received(CB.at[9], y_r.at[2])

    received(RB.at[1, pl.ds(0, 7)], rs_r.at[1])
    drained(RB.at[1, pl.ds(0, 7)], rs_s.at[1])
    for b, came, went in ((0, c > 0, c < 63), (2, c < 63, c > 0)):
        pl.when(came)(lambda b=b: received(RB.at[b], rs_r.at[b]))
        pl.when(went)(lambda b=b: drained(RB.at[b], rs_s.at[b]))
    for t, buf, b, pred in jobs:

        def gone(t=t, buf=buf, b=b):
            pl.when(t == p)(lambda: drained(buf.at[pl.ds(0, 7)], z_s.at[b]))
            pl.when(t != p)(lambda: drained(buf, z_s.at[b]))

        cond(pred, gone)
    for buf, b, owner, member, cslot in spreads:
        cond(member, lambda b=b: drained(CB.at[pl.ds(0, 7)], y_s.at[b]))


def send(src, dst, s, r, dev):
    rcopy(src, dst, s, r, dev).start()


def received(ref, sem):
    rcopy(ref, ref, sem, sem, (0, 0)).wait_recv()


def drained(ref, sem):
    rcopy(ref, ref, sem, sem, (0, 0)).wait_send()


DIST = (1, -1, 2, -2, 3, -3, 4)


class Weights:
    def __init__(self, arrs, place, ss, zr, nr, pr):
        self.arrs = arrs
        self.c, self.p, self.zh, x, y, self.h = place
        self.color = (x + y) % 2
        self.partner = (self.c + 1 - 2 * self.h, self.p)
        self.plane = [
            (ctx_of(self.zh, (x + dx) % 4, (y + dy) % 4, self.h), self.p)
            for dx, dy in ((1, 0), (3, 0), (0, 1), (0, 3))
        ]
        self.ss, self.zr, self.nr, self.pr = ss, zr, nr, pr

    def at(self, d):
        return at_z(self.c, self.zh, self.p, d)

    def quarter(self, i, base, h, color, side=None):
        src, _ = self.arrs[i]
        r, w = src.shape
        if i < 3:
            n = r // 4
            row, lane, wide = base + h * 2 * n + color * n, 0, w
        else:
            n = r // 2
            row, lane, wide = base + h * n, pl.multiple_of(color * (w // 2), w // 2), w // 2
        if side is not None:
            wide = wide // 2
            lane = lane + side * wide
            if i == 3:
                lane = pl.multiple_of(lane, wide)
        return pl.ds(pl.multiple_of(row, n), n), pl.ds(lane, wide)

    def own(self, i, side=None):
        rows, lanes = self.quarter(i, 0, self.h, self.color, side)
        return self.arrs[i][0].at[rows, lanes]

    def part(self, i, m, flip_h=0, flip_c=0, side=None, d=None):
        src, out = self.arrs[i]
        d = DIST[m] if d is None else d
        base = ((self.p - d + 8) % 8) * src.shape[0]
        h = 1 - self.h if flip_h else self.h
        color = 1 - self.color if flip_c else self.color
        rows, lanes = self.quarter(i, base, h, color, side)
        return out.at[rows, lanes]

    def direct(self):
        for m in range(7):
            for i in range(2):
                d = DIST[m] if m < 6 else (4, -4)[i]
                send(self.own(i), self.part(i, m, d=0), self.ss.at[i], self.zr.at[i, m], self.at(d))

    def first(self, i):
        for di, d in enumerate((1, -1)):
            dst = self.part(i, di, d=0)
            send(self.own(i), dst, self.ss.at[i], self.zr.at[i, di], self.at(d))

    def hop(self, i, t):
        for di, d in enumerate((1, -1)):
            m = (t - 1) * 2 + di
            received(self.part(i, m), self.zr.at[i, m])
            ref = self.part(i, m, side=di if t == 3 else None)
            send(ref, ref, self.ss.at[i], self.zr.at[i, min(m + 2, 6)], self.at(d))
            self.spread(i, m)

    def spread(self, i, m):
        ref = self.part(i, m)
        send(ref, ref, self.ss.at[i], self.pr.at[i], self.partner)
        to = self.plane[m % 4]
        send(ref, ref, self.ss.at[i], self.nr.at[i, m], to)

    def take(self, i, m):
        received(self.part(i, m), self.zr.at[i, m])
        self.spread(i, m)

    def near(self, i):
        for m in range(7):
            ref = self.part(i, m, flip_c=1)
            received(ref, self.nr.at[i, m])
            send(ref, ref, self.ss.at[i], self.pr.at[i], self.partner)

    def done(self, i):
        src, out = self.arrs[i]
        received(out.at[pl.ds(0, 7 * src.shape[0] // 2), :], self.pr.at[i])

    def finish(self):
        for i, (src, out) in enumerate(self.arrs):
            drained(out.at[pl.ds(0, 7 * src.shape[0]), :], self.ss.at[i])


class Gather:
    def __init__(self, kv, place, ss, rs, pr):
        self.kv = kv
        c, p, zh, x, y, h = place
        self.ss, self.rs, self.pr = ss, rs, pr
        self.partner = (c + 1 - 2 * h, p)
        self.ap = (ctx_of(zh, (x + 1 - h) % 4, (y + h) % 4, h), p)
        self.am = (ctx_of(zh, (x + 3 + h) % 4, (y + 4 - h) % 4, h), p)
        self.af = (ctx_of(zh, (x + 2 - 2 * h) % 4, (y + 2 * h) % 4, h), p)
        self.bp = (ctx_of(zh, (x + h) % 4, (y + 1 - h) % 4, h), p)
        self.bm = (ctx_of(zh, (x + 4 - h) % 4, (y + 3 + h) % 4, h), p)

    def slot(self, g, j, m, r=0):
        return self.kv.at[((g * 4 + j) * 2 + r) * 4 + m]

    def half(self, g, j, m, k):
        return self.kv.at[((g * 4 + j) * 2) * 4 + m, pl.ds(k * HB, HB), :]

    def got(self, ref, k):
        received(ref, self.rs.at[k])

    def send(self, src, dst, k, dev):
        send(src, dst, self.ss, self.rs.at[k], dev)

    def to_b(self, g, j, src=None):
        src = self.slot(g, j, 0) if src is None else src
        k = 15 * g + 3 + 3 * j
        self.send(src, self.slot(g, j, 1), k, self.bp)
        self.send(src, self.slot(g, j, 2), k + 1, self.bm)

    def to_partner(self, g, j, m, src=None):
        src = self.slot(g, j, m) if src is None else src
        send(src, self.slot(g, j, m, 1), self.ss, self.pr.at[4 * g + j], self.partner)

    def own_a(self, g, src=None):
        a = self.slot(g, 0, 0) if src is None else src
        self.send(a, self.slot(g, 1, 0), 15 * g, self.ap)
        self.send(a, self.slot(g, 2, 0), 15 * g + 1, self.am)

    def own_b(self, g, src=None):
        a = self.slot(g, 0, 0) if src is None else src
        self.send(a, self.slot(g, 3, 0), 15 * g + 2, self.af)
        self.to_b(g, 0, src)
        self.to_partner(g, 0, 0, src)

    def a_near(self, g):
        for j, k in ((1, 0), (2, 1)):
            self.got(self.slot(g, j, 0), 15 * g + k)
            self.to_b(g, j)
            self.to_partner(g, j, 0)

    def a_far(self, g):
        self.got(self.slot(g, 3, 0), 15 * g + 2)
        self.to_b(g, 3)
        self.to_partner(g, 3, 0)

    def b_near(self, g, j):
        base = 15 * g + 3 + 3 * j
        for m, k, dev in ((1, 0, self.bp), (2, 1, self.bm)):
            self.got(self.slot(g, j, m), base + k)
            self.send(self.half(g, j, m, k), self.half(g, j, 3, k), base + 2, dev)
            self.to_partner(g, j, m)

    def b_far(self, g, j):
        self.got(self.slot(g, j, 3), 15 * g + 3 + 3 * j + 2)
        self.to_partner(g, j, 3)

    def from_partner(self, g, j):
        received(self.kv.at[pl.ds(((g * 4 + j) * 2 + 1) * 4, 4)], self.pr.at[4 * g + j])

    def finish(self):
        drained(self.kv, self.ss)


def front_kernel(
    tok_hbm, wk, wv, wq, wo, gain, wpair_hbm,
    seq, RB, CB,
    WK, WV, WQ, WO, tok, wpair, kv, blk, relay, q, acc, high, mixed, line, rb, cb, HM, HL, HR,
    wss, wzr, wnr, wpr, kss, krs, kpr, zr, hr, ls, rs_s, rs_r, z_s, z_r, y_s, y_r,
):
    place = coords()
    c, p, zh, x, y, h = place
    arrs = ((wk, WK), (wv, WV), (wq, WQ), (wo, WO))
    ring = Weights(arrs, place, wss, wzr, wnr, wpr)
    kvs = Gather(kv, place, kss, krs, kpr)
    enter([ring.at(d) for d in (4, -4, 3, -3, 2, -2, 1, -1)] + ring.plane + [ring.partner])
    ring.direct()
    ring.first(2)
    locs = []
    for i, (src, out) in enumerate(arrs):
        r = src.shape[0]
        locs.append((src, out.at[pl.ds(pl.multiple_of(p * r, r), r), :]))
    locs += [(tok_hbm, tok), (wpair_hbm, wpair)]
    locs = [pltpu.make_async_copy(src, dst, ls.at[i]) for i, (src, dst) in enumerate(locs)]
    for cp in locs:
        cp.start()

    for m in range(7):
        ring.take(0, m)
        ring.take(1, m)
        if m == 3:
            ring.hop(2, 1)
    for i in (0, 1, 4):
        locs[i].wait()
    ring.near(0)
    ring.near(1)
    ring.hop(2, 2)
    ring.done(0)
    ring.done(1)
    t = tok[...]
    blk[0:128, :] = jnp.dot(t, WK[...], preferred_element_type=F32).astype(BF)
    v = jnp.dot(t, WV[...], preferred_element_type=F32)
    blk[128:256, :] = v[:, :128].astype(BF)
    blk[256:320, :] = jnp.concatenate([v[0:64, 128:192], v[64:128, 128:192]], axis=1).astype(BF)

    kvs.own_a(0, blk)
    for k in range(2):
        send(blk.at[pl.ds(k * HB, HB), :], relay.at[k], kss, hr.at[k], ring.at((4, -4)[k]))
    kvs.own_b(0, blk)
    ring.first(3)
    loc = pltpu.make_async_copy(blk, kvs.slot(0, 0, 0), ls.at[6])
    loc.start()
    acc[...] = jnp.zeros_like(acc)
    high[...] = jnp.full_like(high, -1e30)
    kvs.a_near(0)
    ring.hop(2, 3)
    kvs.a_far(0)
    kvs.b_near(0, 0)
    for k in range(2):
        received(relay.at[k], hr.at[k])
        send(relay.at[k], kvs.half(1, 0, 0, k), kss, zr, ring.at((4, -4)[k]))
    ring.hop(3, 1)
    kvs.b_near(0, 1)
    kvs.b_near(0, 2)
    kvs.b_far(0, 0)
    ring.take(2, 6)
    kvs.b_near(0, 3)
    received(kvs.slot(1, 0, 0), zr)
    kvs.own_a(1)
    kvs.own_b(1)
    ring.near(2)
    loc.wait()
    locs[2].wait()
    ring.done(2)
    qq = jnp.dot(tok[...], WQ[...], preferred_element_type=F32).astype(BF)
    for n in range(H):
        q[n * 128 : (n + 1) * 128, :] = qq[:, n * KEY : (n + 1) * KEY]

    scale = KEY ** (-0.5) * 1.4426950408889634

    def attend(g, j):
        kvs.from_partner(g, j)
        part = kv[pl.ds((g * 4 + j) * 8, 8)]
        k = part[:, 0:128, :].reshape(1024, 128)
        v1 = part[:, 128:256, :].reshape(1024, 128)
        lo = part[:, 256:320, :].astype(F32)
        hi = pltpu.roll(lo.reshape(512, 128), 64, 1).reshape(8, 64, 128)
        v2 = jnp.concatenate([lo, hi], axis=1).reshape(1024, 128)
        lane = lax.broadcasted_iota(jnp.int32, (1024, 128), 1)
        v2 = jnp.where(lane == 64, 1.0, v2).astype(BF)
        m = high[:, 0:1]
        s = lax.dot_general(q[...], k, (((1,), (1,)), ((), ())), preferred_element_type=F32)
        m2 = jnp.maximum(m, jnp.max(s, axis=1, keepdims=True))
        w = jnp.exp2((s - m2) * scale).astype(BF)
        o = jnp.dot(w, jnp.concatenate([v1, v2], axis=1), preferred_element_type=F32)
        acc[...] = acc[...] * jnp.exp2((m - m2) * scale) + o
        high[...] = jnp.broadcast_to(m2, high.shape)

    attend(0, 0)
    ring.hop(3, 2)
    for j in (1, 2, 3):
        kvs.b_far(0, j)
    kvs.a_near(1)
    kvs.a_far(1)
    kvs.b_near(1, 0)
    attend(0, 1)
    ring.hop(3, 3)
    attend(0, 2)
    kvs.b_near(1, 1)
    kvs.b_near(1, 2)
    kvs.b_far(1, 0)
    attend(0, 3)
    ring.take(3, 6)
    kvs.b_near(1, 3)
    kvs.b_far(1, 1)
    kvs.b_far(1, 2)
    attend(1, 0)
    kvs.b_far(1, 3)
    attend(1, 1)
    ring.near(3)
    attend(1, 2)
    attend(1, 3)
    locs[3].wait()
    locs[5].wait()
    ring.done(3)

    a = acc[...]
    mx = (a[:, 0:VAL] / a[:, VAL : VAL + 1]).astype(BF)
    for n in range(H):
        mixed[:, n * VAL : (n + 1) * VAL] = mx[n * 128 : (n + 1) * 128, :]
    summed = tok[...].astype(F32) + jnp.dot(mixed[...], WO[...], preferred_element_type=F32)
    line[...] = summed.astype(BF)
    keep = pltpu.make_async_copy(line, seq, ls.at[7])
    keep.start()
    pooled = jnp.mean(summed.reshape(8, POOL, summed.shape[1]), axis=1)
    ms = jnp.mean(pooled * pooled, axis=-1, keepdims=True)
    normed = (pooled * lax.rsqrt(ms + 1e-06) * gain[...].reshape(1, -1)).astype(BF)
    both = jnp.dot(normed, wpair[...], preferred_element_type=F32).astype(BF)
    rb[...] = both[:, :PC]
    cb[...] = both[:, PC:]
    exchange(rb, cb, RB, CB, HM, HL, HR, rs_s, rs_r, z_s, z_r, y_s, y_r)
    ring.finish()
    kvs.finish()
    keep.wait()


def front(tok, wk, wv, wq, wo, gain, wpair):
    vm = pl.BlockSpec(memory_space=pltpu.VMEM)
    dma = pltpu.SemaphoreType.DMA
    hold = pltpu.VMEM((8, 8, PC), BF)
    hbm = pl.BlockSpec(memory_space=pl.ANY)
    return pl.pallas_call(
        front_kernel,
        out_shape=(
            jax.ShapeDtypeStruct(tok.shape, BF),
            jax.ShapeDtypeStruct((3, 8, 8, PC), BF),
            jax.ShapeDtypeStruct((10, 8, 8, PC), BF),
        ),
        in_specs=[hbm] * 5 + [vm, hbm],
        out_specs=(hbm, vm, vm),
        scratch_shapes=[pltpu.VMEM((8 * w.shape[0], w.shape[1]), BF) for w in (wk, wv, wq, wo)]
        + [
            pltpu.VMEM(tok.shape, BF),
            pltpu.VMEM(wpair.shape, BF),
            pltpu.VMEM((64, BR, 128), BF),
            pltpu.VMEM((BR, 128), BF),
            pltpu.VMEM((2, HB, 128), BF),
            pltpu.VMEM((512, 128), BF),
            pltpu.VMEM((512, 256), F32),
            pltpu.VMEM((512, 128), F32),
            pltpu.VMEM((128, H * VAL), BF),
            pltpu.VMEM(tok.shape, BF),
            pltpu.VMEM((8, PC), BF),
            pltpu.VMEM((8, PC), BF),
            hold,
            hold,
            hold,
        ]
        + [dma((4,)), dma((4, 7)), dma((4, 7)), dma((4,)), dma, dma((30,)), dma((8,)), dma, dma((2,)), dma((8,))]
        + [dma((3,))] * 6,
        compiler_params=pltpu.CompilerParams(
            collective_id=0, has_side_effects=True, vmem_limit_bytes=VMEM_LIMIT
        ),
        name="front",
    )(tok, wk, wv, wq, wo, gain, wpair)


def conv_kernel(rb, cb, w, seq_in, out, seq_out, tile, line, wide, sems):
    bring = pltpu.make_async_copy(seq_in, line, sems.at[8])
    bring.start()

    for r in range(4):
        for n in range(2):
            a = r - n
            for b in range(3):
                k = (3 * r + b) * PC
                if 0 <= a < 3:
                    tap = (3 * a + b) * PC
                    wide[k : k + PC, n * PC : (n + 1) * PC] = w[tap : tap + PC, :]
                else:
                    wide[k : k + PC, n * PC : (n + 1) * PC] = jnp.zeros((PC, PC), BF)

    def put(s):
        return pltpu.make_async_copy(tile.at[s], out.at[s], sems.at[s])

    first = (0, 4, 1, 5)

    def seq(s):
        prev = rb[0, pl.ds(s, 1)].reshape(8, PC).astype(F32)
        own = rb[1, pl.ds(s, 1)].reshape(8, PC).astype(F32)
        nxt = rb[2, pl.ds(s, 1)].reshape(8, PC).astype(F32)
        col = jnp.concatenate([cb[k, pl.ds(s, 1)].reshape(8, PC) for k in range(10)], axis=0).astype(F32)
        rows = [prev[6:7], prev[7:8]] + [own[k : k + 1] for k in range(8)] + [nxt[0:1], nxt[1:2]]
        shifted = [col[6 + 2 * b : 70 + 2 * b] for b in range(3)]
        maps = [[(r * cs).astype(BF) for r in rows] for cs in shifted]
        lhs = jnp.concatenate(
            [
                jnp.concatenate([maps[b][i + 2 * r] for i in first], axis=0)
                for r in range(4)
                for b in range(3)
            ],
            axis=1,
        )
        t = jnp.dot(lhs, wide[...], preferred_element_type=F32)
        for q, i in enumerate(first):
            for n in range(2):
                conv = t[64 * q : 64 * q + 64, n * PC : (n + 1) * PC]
                res = maps[1][i + 2 * n + 2].astype(F32) + jax.nn.gelu(conv)
                tile[pl.ds(s, 1), i + 2 * n] = res.astype(BF).reshape(1, 64, PC)
        put(s).start()

    def two(n, carry):
        seq(2 * n)
        seq(2 * n + 1)
        return carry

    lax.fori_loop(0, 4, two, 0)
    bring.wait()
    give = pltpu.make_async_copy(line, seq_out, sems.at[8])
    give.start()
    for s in range(8):
        put(s).wait()
    give.wait()


def convolve(rb, cb, w, seq):
    vm = pl.BlockSpec(memory_space=pltpu.VMEM)
    hbm = pl.BlockSpec(memory_space=pl.ANY)
    return pl.pallas_call(
        conv_kernel,
        out_shape=(jax.ShapeDtypeStruct((8, 8, 64, PC), BF), jax.ShapeDtypeStruct(seq.shape, BF)),
        in_specs=[vm] * 3 + [hbm],
        out_specs=(hbm, hbm),
        scratch_shapes=[
            pltpu.VMEM((8, 8, 64, PC), BF),
            pltpu.VMEM(seq.shape, BF),
            pltpu.VMEM((12 * PC, 2 * PC), BF),
            pltpu.SemaphoreType.DMA((9,)),
        ],
        compiler_params=pltpu.CompilerParams(vmem_limit_bytes=VMEM_LIMIT),
        name="convolve",
    )(rb, cb, w, seq)


def on_device(tokens, w_query, w_key, w_value, w_out, norm_gain, w_pair, conv_weight):
    tok = tokens.reshape(tokens.shape[1], tokens.shape[2])
    seq, rb, cb = front(tok, w_key, w_value, w_query, w_out, norm_gain, w_pair)
    out, seq = convolve(rb, cb, conv_weight.reshape(9 * PC, PC), seq)
    return seq.reshape(tokens.shape), out


def solution(mesh):
    return jax.shard_map(
        on_device,
        mesh=mesh,
        in_specs=(
            P("pair", "ctx", None),
            P("pair", None),
            P("pair", None),
            P("pair", None),
            P("pair", None),
            P(),
            P(),
            P(),
        ),
        out_specs=(P("pair", "ctx", None), P(None, "ctx", "pair", None)),
        check_vma=False,
    )
```
